32 devices in a mesh: groups: 2 (over y), ctx: 16 (over z, x, core).
Axes of the slice: x: 2, y: 2, z: 4, core: 2. Of those that a mesh axis runs over, the one named last changes fastest.
Arguments:
- self_qkv: bfloat16 [3, 8192, 2048], P(None, ('groups', 'ctx')), parts along dimension 1, may hold values from -64 to 64
- windows: int32 [16], replicated, may hold values from 256 to 2048, as said below
- k_gain: float32 [2048], replicated, may hold values from 0.25 to 1.75
- cont_qkv: bfloat16 [3, 256, 2048], P(None, ('groups', 'ctx')), parts along dimension 1, may hold values from -64 to 64
- starts: int32 [32], P('groups'), parts along dimension 0, may hold values from 1 to 4096
Outputs:
- self_out: bfloat16 [8192, 2048], P(('groups', 'ctx')), parts along dimension 0
- cross_out: bfloat16 [256, 2048], P(('groups', 'ctx')), parts along dimension 0
The draws below stay inside these ranges and needn't reach their ends.
There are 2 independent parts, one for each index of `groups`. The reference program is written for one: setup_inputs(seed, part) draws one part's arguments, and reference() takes and returns one part's arrays. A program takes and returns all parts, laid end to end along the dimension named above; an argument that names none is the same for every part. Nothing has to cross between parts.
Inputs may be any that keep to these rules, and one draw needn't show every extreme that they name: `windows`: some head has a window of exactly 2048.
All inputs are finite; a program needn't handle non-finite values.
Results may differ from the reference program's by a relative error of at most 0.0055.
Values may be sent and summed in bfloat16 or wider, within the bound.
No kernel may reach another device: no remote copies, remote signals or barrier semaphores. Data moves between devices by JAX's collectives and lax.ppermute only.
A program may use at most 128 MiB of HBM per device.

```python
import math
import jax
import jax.numpy as jnp
from jax import lax

HEADS = 16
HDIM = 128
WIN = 2048
TOK_DEV = 256
CLEN = 8
HD = 2048
TOKENS = 4096
CONTS = 16
ROWS = 128
N_CTX = 16


def draw_self_qkv(key, part):
    shape = (3, TOKENS, HEADS * HDIM)
    values = jnp.clip(jax.random.normal(key, shape, jnp.float32), -6.0, 6.0)
    return values.astype(jnp.bfloat16)


def draw_cont_qkv(key, part):
    shape = (3, ROWS, HEADS * HDIM)
    values = jnp.clip(jax.random.normal(key, shape, jnp.float32), -6.0, 6.0)
    return values.astype(jnp.bfloat16)


def draw_windows(key, part):
    first, second = jax.random.split(key)
    widths = jax.random.randint(first, (HEADS,), max(2, WIN // 8), WIN + 1)
    chosen = jax.random.randint(second, (), 0, HEADS)
    return jnp.where(jnp.arange(HEADS) == chosen, WIN, widths).astype(jnp.int32)


def plant(drawn, rng, least, largest):
    longest = drawn.shape.index(max(drawn.shape))
    spots = []
    for shift in (0, 1):
        where = [jax.random.randint(jax.random.fold_in(rng, axis), (), 0, length) for axis, length in enumerate(drawn.shape)]
        where[longest] = (where[longest] + shift) % drawn.shape[longest]
        spots.append(tuple(where))
    return drawn.at[spots[0]].set(least).at[spots[1]].set(largest)


def setup_inputs(seed: int = 0, part: int = 0) -> dict:
    seeds = jax.random.split(jax.random.key(seed), 6)
    part_splits = jax.random.split(jax.random.fold_in(seeds[5], part), 6)
    self_qkv = draw_self_qkv(jax.random.fold_in(jax.random.fold_in(seeds[5], part), 71), part)
    windows = draw_windows(jax.random.fold_in(seeds[5], 71), part)
    k_gain = jnp.clip(1.0 + 0.15 * jax.random.normal(seeds[2], (HD,), jnp.float32), 0.25, 1.75)
    cont_qkv = draw_cont_qkv(jax.random.fold_in(jax.random.fold_in(seeds[5], part), 71), part)
    starts = plant(jax.random.randint(part_splits[4], (CONTS,), 1, TOKENS + 1), jax.random.fold_in(part_splits[4], 1), 1, TOKENS).astype(jnp.int32)
    return {"self_qkv": self_qkv, "windows": windows, "k_gain": k_gain, "cont_qkv": cont_qkv, "starts": starts}


EPSILON = 1e-06
NEGATIVE = -1e+30

def rounded(values):
    return lax.optimization_barrier(values.astype(jnp.bfloat16)).astype(jnp.float32)

def window_block(queries, keys, values, windows, anchor, length, reach):
    scaling = 1.0 / math.sqrt(queries.shape[-1])
    scores = jnp.einsum('ihd,jhd->hij', queries, keys) * scaling
    width = (reach + 1) * length
    distance = jnp.arange(length, dtype=jnp.int32)[:, None] + reach * length - jnp.arange(width, dtype=jnp.int32)[None, :]
    key_position = anchor - reach * length + jnp.arange(width, dtype=jnp.int32)
    visible = (distance[None] >= 0) & (distance[None] < windows[:, None, None]) & (key_position >= 0)[None, None, :]
    scores = jnp.where(visible, scores, NEGATIVE)
    highest = lax.optimization_barrier(jnp.max(scores, axis=-1, keepdims=True))
    expo = jnp.where(visible, jnp.exp(scores - highest), 0.0)
    weights = rounded(expo / lax.optimization_barrier(jnp.sum(expo, axis=-1, keepdims=True)))
    return jnp.einsum('hij,jhd->ihd', weights, values)

def reference(self_qkv, windows, k_gain, cont_qkv, starts):
    length = TOK_DEV
    reach = WIN // TOK_DEV
    features = HEADS * HDIM
    scaling = 1.0 / math.sqrt(HDIM)
    padding = jnp.zeros((2, reach * length, features), jnp.bfloat16)
    band = jnp.concatenate([padding, self_qkv[1:3]], axis=1)

    def self_block(block_index):
        anchor = (block_index * length).astype(jnp.int32)
        queries = lax.dynamic_slice_in_dim(self_qkv[0], anchor, length, 0).astype(jnp.float32).reshape(length, HEADS, HDIM)
        key_value = lax.dynamic_slice_in_dim(band, anchor, (reach + 1) * length, 1).astype(jnp.float32).reshape(2, (reach + 1) * length, HEADS, HDIM)
        attended = window_block(queries, key_value[0], key_value[1], windows, anchor, length, reach)
        return attended.reshape(length, features).astype(jnp.bfloat16)
    self_out = lax.map(self_block, jnp.arange(N_CTX, dtype=jnp.int32)).reshape(TOKENS, features)
    hidden = self_out.astype(jnp.float32).reshape(TOKENS, HEADS, HDIM)
    normed = hidden * lax.rsqrt(lax.optimization_barrier(jnp.mean(hidden * hidden, axis=-1, keepdims=True)) + EPSILON)
    cache_keys = (normed.reshape(TOKENS, features) * k_gain).astype(jnp.bfloat16)
    key_blocks = cache_keys.reshape(N_CTX, length, HEADS, HDIM)
    value_blocks = self_out.reshape(N_CTX, length, HEADS, HDIM)
    queries = cont_qkv[0].astype(jnp.float32).reshape(ROWS, HEADS, HDIM)
    row_start = jnp.broadcast_to(starts[:, None], (CONTS, CLEN)).reshape(ROWS)

    def step(carry, inputs):
        highest, totals, weighted = carry
        block_index, key_block, value_block = inputs
        positions = block_index * length + jnp.arange(length, dtype=jnp.int32)
        visible = (positions[None, :] < row_start[:, None])[None]
        scores = jnp.einsum('ihd,jhd->hij', queries, key_block.astype(jnp.float32)) * scaling
        scores = jnp.where(visible, scores, NEGATIVE)
        new_high = jnp.maximum(highest, lax.optimization_barrier(jnp.max(scores, axis=-1)))
        rescale = jnp.exp(highest - new_high)
        expo = jnp.where(visible, jnp.exp(scores - new_high[..., None]), 0.0)
        totals = rescale * totals + lax.optimization_barrier(jnp.sum(expo, axis=-1))
        weighted = weighted * rescale.T[..., None] + jnp.einsum('hij,jhd->ihd', rounded(expo), value_block.astype(jnp.float32))
        return ((new_high, totals, weighted), None)
    initial = (jnp.full((HEADS, ROWS), NEGATIVE, jnp.float32), jnp.zeros((HEADS, ROWS), jnp.float32), jnp.zeros((ROWS, HEADS, HDIM), jnp.float32))
    (highest, totals, weighted), _ = lax.scan(step, initial, (jnp.arange(N_CTX, dtype=jnp.int32), key_blocks, value_blocks))
    parts = cont_qkv.astype(jnp.float32).reshape(3, CONTS, CLEN, HEADS, HDIM)
    scores = jnp.einsum('cihd,cjhd->hcij', parts[0], parts[1]) * scaling
    causal = (jnp.arange(CLEN)[None, :] <= jnp.arange(CLEN)[:, None])[None, None]
    scores = jnp.where(causal, scores, NEGATIVE)
    prior_high = highest.reshape(HEADS, CONTS, CLEN)
    final = jnp.maximum(prior_high, lax.optimization_barrier(jnp.max(scores, axis=-1)))
    rescale = jnp.exp(prior_high - final)
    expo = jnp.where(causal, jnp.exp(scores - final[..., None]), 0.0)
    all_totals = rescale * totals.reshape(HEADS, CONTS, CLEN) + lax.optimization_barrier(jnp.sum(expo, axis=-1))
    own_sum = jnp.einsum('hcij,cjhd->cihd', rounded(expo), parts[2])
    merged = weighted.reshape(CONTS, CLEN, HEADS, HDIM) * jnp.transpose(rescale, (1, 2, 0))[..., None] + own_sum
    result = merged / jnp.transpose(all_totals, (1, 2, 0))[..., None]
    cross_out = result.reshape(ROWS, features).astype(jnp.bfloat16)
    return (self_out, cross_out)
```

```python
import functools
import math

import jax
import jax.numpy as jnp
from jax import lax
from jax.experimental import pallas as pl
from jax.experimental.pallas import tpu as pltpu
from jax.sharding import PartitionSpec as P


WIN = 2048
CLEN = 8

EPSILON = 1e-06
NEGATIVE = -1e30
FLOOR = -1e29
BF16 = jnp.bfloat16
F32 = jnp.float32

SMEM = pl.BlockSpec(memory_space=pltpu.SMEM)
VMEM = pl.BlockSpec(memory_space=pltpu.VMEM)
ANY = pl.BlockSpec(memory_space=pl.ANY)


def cost(micros):
    return pl.CostEstimate(flops=int(micros * 1.15e9), bytes_accessed=0, transcendentals=0)


def pieces(value):
    high = value.astype(BF16)
    rest = value - high.astype(F32)
    middle = rest.astype(BF16)
    low = (rest - middle.astype(F32)).astype(BF16)
    return high, middle, low


def dot(left, right, contract):
    return lax.dot_general(left, right, ((contract[:1], contract[1:]), ((), ())), preferred_element_type=F32)


def lanes(head, head_dim):
    return pl.ds(pl.multiple_of(head * head_dim, head_dim), head_dim)


def pack_kernel(dims, axis, order, qkv, *outs):
    group, slots, near, head_dim = dims
    step = pl.program_id(0)
    far = slots - near
    mine = lax.rem(lax.axis_index(axis), group)
    for k in range(group):
        kv_far, q_near, rest = outs[k], outs[group + k], outs[2 * group + k]
        first = jnp.bitwise_xor(mine, k) * slots

        def move(target, spot, start, heads):
            for c in range(heads):
                column = slice(c * head_dim, (c + 1) * head_dim)
                target[spot + (slice(None), column)] = qkv[0, :, lanes(order[start + c], head_dim)]

        @pl.when(step == 2)
        def _():
            move(q_near, (), first, near)
            move(rest, (0,), first + near, far)

        @pl.when(step < 2)
        def _():
            move(rest, (0,), first, near)
            move(kv_far, (0,), first + near, far)


def gather_kernel(axis, *refs):
    group = len(refs) - 2
    blocks, out, sems = refs[:group], refs[group], refs[group + 1]
    mine = lax.rem(lax.axis_index(axis), group)
    copies = [
        pltpu.make_async_copy(block, out.at[jnp.bitwise_xor(mine, k)], sems.at[k]) for k, block in enumerate(blocks)
    ]
    for copy in copies:
        copy.start()
    for copy in copies:
        copy.wait()


def pack_rows_kernel(dims, order, rows, out):
    group, slots, _, head_dim = dims
    for device in range(out.shape[0]):
        for c in range(slots):
            out[device, :, c * head_dim : (c + 1) * head_dim] = rows[
                0, :, lanes(order[(device % group) * slots + c], head_dim)
            ]


def attend(kv, queries, window, head, part, base, high_limit, key_parts, state, block, head_dim):
    peak, total, acc = state
    shards = block // kv.shape[2]
    factor = math.log2(math.e) / math.sqrt(head_dim)
    column = lanes(head, head_dim)
    row_index = lax.broadcasted_iota(jnp.int32, (block, block), 1)
    key_index = lax.broadcasted_iota(jnp.int32, (block, block), 0)

    def step(distance, diagonal):
        spot = pl.ds((base + part - distance) * shards, shards)
        keys = kv[spot, 0, :, column].reshape(block, head_dim)
        values = kv[spot, 1, :, column].reshape(block, head_dim)
        q = queries[pl.ds(part * shards, shards), :, column].reshape(block, head_dim)
        scores = dot(keys, q, (1, 1))
        gap = row_index - key_index
        visible = gap < window - distance * block
        if diagonal:
            visible = visible & (gap >= 0)
        scores = jnp.where(visible, scores, NEGATIVE)
        old = peak[0:1, :]
        new = jnp.maximum(old, jnp.max(scores, axis=0, keepdims=True))
        fade = jnp.exp2((old - new) * factor)
        expo = jnp.exp2((scores - new) * factor)
        total[0:1, :] = total[0:1, :] * fade + jnp.sum(expo, axis=0, keepdims=True)
        peak[0:1, :] = new
        acc[...] = acc[...] * fade + dot(values, expo.astype(BF16), (0, 0))

    reach = jnp.minimum((window + block - 2) // block, high_limit)
    low = jnp.maximum(base + part - (key_parts - 1), 0)

    if base - (key_parts - 1) <= 0:

        @pl.when(low == 0)
        def _():
            step(0, True)

    def loop(distance, carry):
        step(distance, False)
        return carry

    lax.fori_loop(jnp.maximum(low, 1), jnp.minimum(reach, base + part) + 1, loop, 0)


def cross_part(out, rows, starts, gain, order, first, offset, anchor, result, head_dim, base=0):
    heads = out.shape[2] // head_dim
    keys_here = out.shape[0] * out.shape[1]
    clen = rows.shape[1]
    devices = rows.shape[0]
    block = min(devices * clen, 128)
    per = block // clen
    factor = math.log2(math.e) / math.sqrt(head_dim)
    tail = slice(base + heads * head_dim, base + (heads + 1) * head_dim)
    for c in range(heads):
        column = slice(c * head_dim, (c + 1) * head_dim)
        values = out[:, :, column].reshape(keys_here, head_dim)
        hidden = values.astype(F32)
        norm = hidden * lax.rsqrt(jnp.mean(hidden * hidden, axis=-1, keepdims=True) + EPSILON)
        keys = (norm * gain[pl.ds(order[first + c], 1), :]).astype(BF16)

        def blocks(index, carry):
            spot = pl.ds(index * per, per)
            q = rows[spot, :, offset + c * head_dim : offset + (c + 1) * head_dim].reshape(block, head_dim)
            scores = dot(q, keys, (1, 1))
            position = anchor + lax.broadcasted_iota(jnp.int32, (block, keys_here), 1)
            seen = position < starts[pl.ds(index * block, block), :]
            scores = jnp.where(seen, scores, NEGATIVE)
            high = jnp.maximum(jnp.max(scores, axis=1, keepdims=True), FLOOR)
            expo = jnp.exp2((scores - high) * factor)
            total = jnp.sum(expo, axis=1, keepdims=True)
            summed = dot(expo.astype(BF16), values, (1, 0))
            result[spot, :, base + c * head_dim : base + (c + 1) * head_dim] = summed.astype(BF16).reshape(
                per, clen, head_dim
            )
            lane = lax.broadcasted_iota(jnp.int32, (block, head_dim), 1)
            stats = jnp.zeros((block, head_dim), F32) if c == 0 else None
            for k, piece in enumerate(pieces(high) + pieces(total)):
                value = jnp.broadcast_to(piece.astype(F32), (block, head_dim))
                if stats is None:
                    stats = result[spot, :, tail].reshape(block, head_dim).astype(F32)
                stats = jnp.where(lane == c * 6 + k, value, stats)
            result[spot, :, tail] = stats.astype(BF16).reshape(per, clen, head_dim)
            return carry

        lax.fori_loop(0, devices * clen // block, blocks, 0)


def scatter_blocks(axis, value, outs):
    mine = lax.rem(lax.axis_index(axis), len(outs))
    for k, out in enumerate(outs):
        out[...] = value[jnp.bitwise_xor(mine, k)]


def reset(peak, total, acc):
    peak[...] = jnp.full(peak.shape, FLOOR, F32)
    total[...] = jnp.zeros(total.shape, F32)
    acc[...] = jnp.zeros(acc.shape, F32)


def far_kernel(dims, axis, order, windows, q, kv0, kv1, kv2, rows, starts, gain, *refs):
    group, slots, near, head_dim, block = dims
    outs, (result, out, kv, peak, total, acc, sems) = refs[:group], refs[group:]
    device = lax.axis_index(axis)
    row = device // group
    mine = lax.rem(device, group) * slots + near
    copies = [
        pltpu.make_async_copy(source, kv.at[pl.ds(k * group, group)], sems.at[k])
        for k, source in enumerate((kv2, kv1, kv0))
    ]
    for copy in copies:
        copy.start()
    for copy in copies:
        copy.wait()
    length = out.shape[1]
    parts = group * length // block
    shards = block // length

    def one(index, carry):
        head = index // parts
        part = lax.rem(index, parts)
        window = windows[order[mine + head]]
        reset(peak, total, acc)
        attend(
            kv, q, window, head, part, 2 * parts, row * parts + part, 3 * parts, (peak, total, acc), block, head_dim
        )
        done = (acc[...] / total[0:1, :]).astype(BF16).T
        out[pl.ds(part * shards, shards), :, lanes(head, head_dim)] = done.reshape(shards, length, head_dim)
        return carry

    lax.fori_loop(0, parts * (slots - near), one, 0)
    scatter_blocks(axis, out, outs)
    cross_part(out, rows, starts, gain, order, mine, near * head_dim, row * group * length, result, head_dim)


def near_kernel(dims, axis, delta, count, order, windows, q, kv, *refs):
    group, slots, near, head_dim, block = dims
    device = lax.axis_index(axis)
    row = device // group
    mine = lax.rem(device, group) * slots
    length = q.shape[1]
    parts = group * length // block
    if delta == 2:
        state, peak, total, acc = refs
    else:
        sums, stats_out, peak, total, acc = refs

    def one(index, carry):
        head = index // parts
        part = lax.rem(index, parts)
        window = windows[order[mine + head]]
        span = pl.ds(pl.multiple_of(part * block, block), block)
        reset(peak, total, acc)
        limit = jnp.where(row + delta < count, 2 * WIN, -1) if delta > 0 else 2 * WIN
        attend(kv, q, window, head, part, delta * parts, limit, parts, (peak, total, acc), block, head_dim)
        if delta == 2:
            write_state(state, head, span, peak[0:1, :], total[0:1, :], acc[...], head_dim)
        else:
            sums[head, :, span] = acc[...]
            stats_out[head, 0:1, span] = peak[0:1, :]
            stats_out[head, 1:2, span] = total[0:1, :]
        return carry

    lax.fori_loop(0, parts * near, one, 0)


def write_state(state, head, span, peak, total, acc, head_dim):
    state[head, 0:head_dim, span] = acc.astype(BF16)
    width = peak.shape[1]
    index = lax.broadcasted_iota(jnp.int32, (16, width), 0)
    stats = jnp.zeros((16, width), F32)
    for k, piece in enumerate(pieces(peak) + pieces(total)):
        stats = jnp.where(index == k, piece.astype(F32), stats)
    state[head, head_dim : head_dim + 16, span] = stats.astype(BF16)


def merged_state(state, sums, stats, head, span, valid, head_dim):
    factor = math.log2(math.e) / math.sqrt(head_dim)
    arrived = state[head, head_dim : head_dim + 16, span].astype(F32)
    far_peak = jnp.where(valid, arrived[0:1] + arrived[1:2] + arrived[2:3], FLOOR)
    far_total = jnp.where(valid, arrived[3:4] + arrived[4:5] + arrived[5:6], 0.0)
    peak, total = stats[head, 0:1, span], stats[head, 1:2, span]
    high = jnp.maximum(peak, far_peak)
    here = jnp.exp2((peak - high) * factor)
    there = jnp.where(valid, jnp.exp2((far_peak - high) * factor), 0.0)
    acc = sums[head, :, span] * here
    arrived_sum = jnp.where(valid, state[head, 0:head_dim, span].astype(F32), 0.0)
    return high, total * here + far_total * there, acc + arrived_sum * there


def merge_kernel(dims, axis, arrived, sums, stats, state):
    group, _, near, head_dim, block = dims
    valid = lax.axis_index(axis) // group >= 1
    width = sums.shape[2]

    def one(index, carry):
        head = index // (width // block)
        span = pl.ds(pl.multiple_of(lax.rem(index, width // block) * block, block), block)
        peak, total, acc = merged_state(arrived, sums, stats, head, span, valid, head_dim)
        write_state(state, head, span, peak, total, acc, head_dim)
        return carry

    lax.fori_loop(0, near * (width // block), one, 0)


def last_kernel(dims, axis, order, arrived, sums, stats, rows, starts, gain, other, *refs):
    group, slots, near, head_dim, block = dims
    outs, (result, out) = refs[:group], refs[group:]
    row = lax.axis_index(axis) // group
    mine = lax.rem(lax.axis_index(axis), group) * slots
    length = out.shape[1]
    parts = group * length // block
    shards = block // length

    def one(index, carry):
        head = index // parts
        part = lax.rem(index, parts)
        span = pl.ds(pl.multiple_of(part * block, block), block)
        _, total, acc = merged_state(arrived, sums, stats, head, span, row >= 1, head_dim)
        done = (acc / total).astype(BF16).T
        out[pl.ds(part * shards, shards), :, lanes(head, head_dim)] = done.reshape(shards, length, head_dim)
        return carry

    lax.fori_loop(0, parts * near, one, 0)
    scatter_blocks(axis, out, outs)
    width = other.shape[2]
    result[:, :, 0:width] = other[...]
    cross_part(
        out, rows, starts, gain, order, mine, 0, row * group * length, result, head_dim, base=width
    )


def finish_kernel(dims, axis, order, cross, cont, *refs):
    group, slots, near, head_dim = dims
    far_out, near_out, (self_out, cross_out) = refs[:group], refs[group : 2 * group], refs[2 * group :]
    mine = lax.rem(lax.axis_index(axis), group)
    far = slots - near
    for k in range(group):
        first = jnp.bitwise_xor(mine, k) * slots
        for slot in range(slots):
            source, c = (near_out, slot) if slot < near else (far_out, slot - near)
            self_out[:, lanes(order[first + slot], head_dim)] = source[k][:, c * head_dim : (c + 1) * head_dim]
    factor = math.log2(math.e) / math.sqrt(head_dim)
    clen = cont.shape[1]
    row_index = lax.broadcasted_iota(jnp.int32, (clen, clen), 0)
    key_index = lax.broadcasted_iota(jnp.int32, (clen, clen), 1)
    visible = (key_index <= row_index) & (key_index // CLEN == row_index // CLEN)
    for g in range(group):
        for slot in range(slots):
            column = lanes(order[g * slots + slot], head_dim)
            base, c, heads = ((far + 1) * head_dim, slot, near) if slot < near else (0, slot - near, far)
            tail = base + heads * head_dim
            stats = cross[:, g, :, tail : tail + head_dim].astype(F32)
            k = 6 * c
            high = stats[:, :, k : k + 1] + stats[:, :, k + 1 : k + 2] + stats[:, :, k + 2 : k + 3]
            total = stats[:, :, k + 3 : k + 4] + stats[:, :, k + 4 : k + 5] + stats[:, :, k + 5 : k + 6]
            scores = jnp.where(visible, dot(cont[0, :, column], cont[1, :, column], (1, 1)), NEGATIVE)
            final = jnp.maximum(jnp.max(high, axis=0), jnp.max(scores, axis=1, keepdims=True))
            weight = jnp.exp2((high - final[None]) * factor)
            expo = jnp.exp2((scores - final) * factor)
            own = dot(expo.astype(BF16), cont[2, :, column], (1, 0))
            denominator = jnp.sum(weight * total, axis=0) + jnp.sum(expo, axis=1, keepdims=True)
            summed = cross[:, g, :, base + c * head_dim : base + (c + 1) * head_dim].astype(F32) * weight
            merged = jnp.sum(summed, axis=0) + own
            cross_out[:, column] = (merged / denominator).astype(BF16)


def per_device(self_qkv, windows, k_gain, cont_qkv, starts):
    axis = "ctx"
    length, features = self_qkv.shape[1:]
    head_count = windows.shape[0]
    head_dim = features // head_count
    devices = lax.axis_size(axis)
    group = WIN // (2 * length)
    slots = head_count // group
    near = slots // 2
    far = slots - near
    count = devices // group
    block = 2 * length
    rows_here = cont_qkv.shape[1]
    rows_all = rows_here * devices
    nearby, distant = near * head_dim, far * head_dim
    dims = (group, slots, near, head_dim)
    big = dims + (block,)
    index = jnp.arange(head_count, dtype=jnp.int32)
    above = (windows[None, :] > windows[:, None]) | (
        (windows[None, :] == windows[:, None]) & (index[None, :] < index[:, None])
    )
    rank = jnp.sum(above.astype(jnp.int32), axis=1)
    place = lax.rem(rank, group) * slots + rank // group
    order = jnp.sum(jnp.where(place[None, :] == index[:, None], index[None, :], 0), axis=1)

    def exchange(blocks):
        got = [blocks[0]]
        for k in range(1, group):
            got.append(lax.ppermute(blocks[k], axis, [(source, source ^ k) for source in range(devices)]))
        return got

    def gather(blocks, micros):
        return pl.pallas_call(
            functools.partial(gather_kernel, axis),
            out_shape=jax.ShapeDtypeStruct((group,) + blocks[0].shape, BF16),
            in_specs=[ANY] * group,
            out_specs=VMEM,
            scratch_shapes=[pltpu.SemaphoreType.DMA((group,))],
            cost_estimate=cost(micros),
        )(*blocks)

    def up(value):
        return lax.ppermute(value, axis, [(k, k + group) for k in range(devices - group)])

    def down(value):
        return lax.ppermute(value, axis, [(k + group, k) for k in range(devices - group)])

    def call(kernel, micros, shapes, *operands, smem=2, **more):
        return pl.pallas_call(
            kernel,
            out_shape=shapes,
            in_specs=[SMEM] * smem + [VMEM] * (len(operands) - smem),
            out_specs=jax.tree.map(lambda _: VMEM, shapes),
            cost_estimate=cost(micros),
            **more,
        )(*operands)

    def shape(*sizes, dtype=BF16):
        return jax.ShapeDtypeStruct(sizes, dtype)

    packed = pl.pallas_call(
        functools.partial(pack_kernel, dims, axis),
        grid=(3, 2),
        out_shape=(shape(2, length, distant),) * group
        + (shape(length, nearby),) * group
        + (shape(3, length, nearby),) * group,
        in_specs=[SMEM, pl.BlockSpec((1, length // 2, features), lambda i, j: (lax.rem(i + 1, 3), j, 0))],
        out_specs=(
            pl.BlockSpec(
                (1, length // 2, distant), lambda i, j: (jnp.minimum(i, 1), jnp.where(i < 2, j, 1), 0)
            ),
        )
        * group
        + (pl.BlockSpec((length // 2, nearby), lambda i, j: (jnp.where(i < 2, 0, j), 0)),) * group
        + (pl.BlockSpec((1, length // 2, nearby), lambda i, j: (i, j, 0)),) * group,
        name="pack",
        cost_estimate=cost(4),
    )(order, self_qkv)
    q_near0 = gather(exchange(packed[group : 2 * group]), 1)
    kv_far0 = gather(exchange(packed[:group]), 2)
    rest0 = gather(exchange(packed[2 * group :]), 2)
    rows_sent = call(
        functools.partial(pack_rows_kernel, dims), 2, shape(devices, rows_here, slots * head_dim), order,
        cont_qkv, smem=1,
    )
    rows = lax.all_to_all(rows_sent, axis, 0, 0, tiled=True)
    row_starts = jnp.broadcast_to(starts[:, None], (starts.shape[0], rows_all // starts.shape[0])).reshape(rows_all, 1)
    gain = k_gain.reshape(head_count, head_dim)

    kv_far1 = up(kv_far0)
    q_near1 = down(q_near0)
    kv_far2 = up(kv_far1)
    q_near2 = down(q_near1)

    state_scratch = [
        pltpu.VMEM((8, block), F32),
        pltpu.VMEM((8, block), F32),
        pltpu.VMEM((head_dim, block), F32),
    ]
    state_shape = shape(near, head_dim + 16, group * length)
    local_shape = (shape(near, head_dim, group * length, dtype=F32), shape(near, 8, group * length, dtype=F32))

    def near_step(delta, q):
        return call(
            functools.partial(near_kernel, big, axis, delta, count), 7,
            state_shape if delta == 2 else local_shape, order, windows, q, rest0, scratch_shapes=state_scratch,
        )

    def merge(kernel, micros, shapes, *operands, **more):
        return call(functools.partial(kernel, big, axis), micros, shapes, *operands, **more)

    state2 = up(near_step(2, q_near2))
    state1 = up(merge(merge_kernel, 1, state_shape, state2, *near_step(1, q_near1), smem=0))
    local0 = near_step(0, q_near0)

    *far_out, far_cross = pl.pallas_call(
        functools.partial(far_kernel, big, axis),
        out_shape=(shape(length, distant),) * group + (shape(devices, rows_here, distant + head_dim),),
        in_specs=[SMEM, SMEM, VMEM, ANY, ANY, ANY, VMEM, VMEM, VMEM],
        out_specs=(VMEM,) * (group + 1),
        scratch_shapes=[pltpu.VMEM((group, length, distant), BF16), pltpu.VMEM((3 * group, 2, length, distant), BF16)]
        + state_scratch
        + [pltpu.SemaphoreType.DMA((3,))],
        name="far",
        cost_estimate=cost(14),
    )(order, windows, rest0[:, 2], kv_far0, kv_far1, kv_far2, rows, row_starts, gain)
    far_back = exchange(far_out)
    *near_out, cross = merge(
        last_kernel, 4,
        (shape(length, nearby),) * group + (shape(devices, rows_here, distant + nearby + 2 * head_dim),),
        order, state1, *local0, rows, row_starts, gain, far_cross, smem=1,
        scratch_shapes=[pltpu.VMEM((group, length, nearby), BF16)],
    )
    near_back = exchange(near_out)
    cross = lax.all_to_all(cross, axis, 0, 0, tiled=True).reshape((count, group) + cross.shape[1:])
    return call(
        functools.partial(finish_kernel, dims, axis), 4, (shape(length, features), shape(rows_here, features)),
        order, cross, cont_qkv, *far_back, *near_back, smem=1,
    )


def solution(mesh):
    in_specs = (
        P(None, ("groups", "ctx"), None),
        P(),
        P(),
        P(None, ("groups", "ctx"), None),
        P("groups"),
    )
    out_specs = (P(("groups", "ctx"), None), P(("groups", "ctx"), None))

    return jax.shard_map(per_device, mesh=mesh, in_specs=in_specs, out_specs=out_specs, check_vma=False)
```

```python
import functools
import math

import jax
import jax.numpy as jnp
from jax import lax
from jax.experimental import pallas as pl
from jax.experimental.pallas import tpu as pltpu
from jax.sharding import PartitionSpec as P


WIN = 2048
CLEN = 8

EPSILON = 1e-06
NEGATIVE = -1e30
FLOOR = -1e29
BF16 = jnp.bfloat16
F32 = jnp.float32

SMEM = pl.BlockSpec(memory_space=pltpu.SMEM)
VMEM = pl.BlockSpec(memory_space=pltpu.VMEM)
ANY = pl.BlockSpec(memory_space=pl.ANY)


def cost(micros):
    return pl.CostEstimate(flops=int(micros * 1.15e9), bytes_accessed=0, transcendentals=0)


def pieces(value):
    high = value.astype(BF16)
    rest = value - high.astype(F32)
    middle = rest.astype(BF16)
    low = (rest - middle.astype(F32)).astype(BF16)
    return high, middle, low


def dot(left, right, contract):
    return lax.dot_general(left, right, ((contract[:1], contract[1:]), ((), ())), preferred_element_type=F32)


def lanes(head, head_dim):
    return pl.ds(pl.multiple_of(head * head_dim, head_dim), head_dim)


def pack_kernel(dims, axis, order, qkv, *outs):
    group, slots, near, head_dim = dims
    step = pl.program_id(0)
    far = slots - near
    mine = lax.rem(lax.axis_index(axis), group)
    for k in range(group):
        kv_far, q_near, rest = outs[k], outs[group + k], outs[2 * group + k]
        first = jnp.bitwise_xor(mine, k) * slots

        def move(target, spot, start, heads):
            for c in range(heads):
                column = slice(c * head_dim, (c + 1) * head_dim)
                target[spot + (slice(None), column)] = qkv[0, :, lanes(order[start + c], head_dim)]

        @pl.when(step == 2)
        def _():
            move(q_near, (), first, near)
            move(rest, (0,), first + near, far)

        @pl.when(step < 2)
        def _():
            move(rest, (0,), first, near)
            move(kv_far, (0,), first + near, far)


def gather_kernel(axis, *refs):
    group = len(refs) - 2
    blocks, out, sems = refs[:group], refs[group], refs[group + 1]
    mine = lax.rem(lax.axis_index(axis), group)
    copies = [
        pltpu.make_async_copy(block, out.at[jnp.bitwise_xor(mine, k)], sems.at[k]) for k, block in enumerate(blocks)
    ]
    for copy in copies:
        copy.start()
    for copy in copies:
        copy.wait()


def pack_rows_kernel(dims, order, rows, out):
    group, slots, _, head_dim = dims
    for device in range(out.shape[0]):
        for c in range(slots):
            out[device, :, c * head_dim : (c + 1) * head_dim] = rows[
                0, :, lanes(order[(device % group) * slots + c], head_dim)
            ]


def attend(kv, queries, windows, part, base, high_limit, key_parts, state, block, head_dim):
    peak, total, acc = state
    shards = block // kv.shape[2]
    factor = math.log2(math.e) / math.sqrt(head_dim)
    row_index = lax.broadcasted_iota(jnp.int32, (block, block), 1)
    key_index = lax.broadcasted_iota(jnp.int32, (block, block), 0)

    def step(distance, diagonal):
        spot = pl.ds((base + part - distance) * shards, shards)
        for head, window in enumerate(windows):
            column = slice(head * head_dim, (head + 1) * head_dim)
            keys = kv[spot, 0, :, column].reshape(block, head_dim)
            values = kv[spot, 1, :, column].reshape(block, head_dim)
            q = queries(part * shards, shards, column).reshape(block, head_dim)
            scores = dot(keys, q, (1, 1))
            visible = row_index < key_index + (window - distance * block)
            if diagonal:
                visible = visible & (row_index >= key_index)
            scores = jnp.where(visible, scores, NEGATIVE)
            old = peak[head, 0:1, :]
            new = jnp.maximum(old, jnp.max(scores, axis=0, keepdims=True))
            fade = jnp.exp2((old - new) * factor)
            expo = jnp.exp2((scores - new) * factor)
            total[head, 0:1, :] = total[head, 0:1, :] * fade + jnp.sum(expo, axis=0, keepdims=True)
            peak[head, 0:1, :] = new
            acc[head] = acc[head] * fade + dot(values, expo.astype(BF16), (0, 0))

    longest = functools.reduce(jnp.maximum, windows)
    reach = jnp.minimum((longest + block - 2) // block, high_limit)
    low = jnp.maximum(base + part - (key_parts - 1), 0)

    if base - (key_parts - 1) <= 0:

        @pl.when(low == 0)
        def _():
            step(0, True)

    def loop(distance, carry):
        step(distance, False)
        return carry

    lax.fori_loop(jnp.maximum(low, 1), jnp.minimum(reach, base + part) + 1, loop, 0)


def cross_part(out, rows, starts, gain, order, first, offset, anchor, result, head_dim, base=0):
    heads = out.shape[2] // head_dim
    keys_here = out.shape[0] * out.shape[1]
    clen = rows.shape[1]
    devices = rows.shape[0]
    block = min(devices * clen, 128)
    per = block // clen
    factor = math.log2(math.e) / math.sqrt(head_dim)
    tail = slice(base + heads * head_dim, base + (heads + 1) * head_dim)
    for c in range(heads):
        column = slice(c * head_dim, (c + 1) * head_dim)
        values = out[:, :, column].reshape(keys_here, head_dim)
        hidden = values.astype(F32)
        norm = hidden * lax.rsqrt(jnp.mean(hidden * hidden, axis=-1, keepdims=True) + EPSILON)
        keys = (norm * gain[pl.ds(order[first + c], 1), :]).astype(BF16)

        def blocks(index, carry):
            spot = pl.ds(index * per, per)
            q = rows[spot, :, offset + c * head_dim : offset + (c + 1) * head_dim].reshape(block, head_dim)
            scores = dot(q, keys, (1, 1))
            position = anchor + lax.broadcasted_iota(jnp.int32, (block, keys_here), 1)
            seen = position < starts[pl.ds(index * block, block), :]
            scores = jnp.where(seen, scores, NEGATIVE)
            high = jnp.maximum(jnp.max(scores, axis=1, keepdims=True), FLOOR)
            expo = jnp.exp2((scores - high) * factor)
            total = jnp.sum(expo, axis=1, keepdims=True)
            summed = dot(expo.astype(BF16), values, (1, 0))
            result[spot, :, base + c * head_dim : base + (c + 1) * head_dim] = summed.astype(BF16).reshape(
                per, clen, head_dim
            )
            lane = lax.broadcasted_iota(jnp.int32, (block, head_dim), 1)
            stats = jnp.zeros((block, head_dim), F32) if c == 0 else None
            for k, piece in enumerate(pieces(high) + pieces(total)):
                value = jnp.broadcast_to(piece.astype(F32), (block, head_dim))
                if stats is None:
                    stats = result[spot, :, tail].reshape(block, head_dim).astype(F32)
                stats = jnp.where(lane == c * 6 + k, value, stats)
            result[spot, :, tail] = stats.astype(BF16).reshape(per, clen, head_dim)
            return carry

        lax.fori_loop(0, devices * clen // block, blocks, 0)


def scatter_blocks(axis, value, outs):
    mine = lax.rem(lax.axis_index(axis), len(outs))
    for k, out in enumerate(outs):
        out[...] = value[jnp.bitwise_xor(mine, k)]


def reset(peak, total, acc):
    peak[...] = jnp.full(peak.shape, FLOOR, F32)
    total[...] = jnp.zeros(total.shape, F32)
    acc[...] = jnp.zeros(acc.shape, F32)


def far_kernel(dims, axis, order, windows, rest, kv0, kv1, kv2, kv3, rows, starts, gain, *refs):
    group, slots, near, head_dim, block = dims
    outs, (result, out, kv, peak, total, acc, sems) = refs[:group], refs[group:]
    device = lax.axis_index(axis)
    row = device // group
    mine = lax.rem(device, group) * slots + near
    copies, start = [], 0
    for k, source in enumerate((kv3, kv2, kv1, kv0)):
        copies.append(pltpu.make_async_copy(source, kv.at[pl.ds(start, source.shape[0])], sems.at[k]))
        start += source.shape[0]
    for copy in copies:
        copy.start()
    for copy in copies:
        copy.wait()
    length = out.shape[1]
    parts = group * length // block
    shards = block // length

    heads = slots - near
    spans = [windows[order[mine + head]] for head in range(heads)]

    def pick(start, size, column):
        return rest[pl.ds(start, size), 2, :, column]

    def one(part, carry):
        reset(peak, total, acc)
        attend(kv, pick, spans, part, 2 * parts, row * parts + part, 3 * parts, (peak, total, acc), block, head_dim)
        for head in range(heads):
            done = (acc[head] / total[head, 0:1, :]).astype(BF16).T
            column = slice(head * head_dim, (head + 1) * head_dim)
            out[pl.ds(part * shards, shards), :, column] = done.reshape(shards, length, head_dim)
        return carry

    lax.fori_loop(0, parts, one, 0)
    scatter_blocks(axis, out, outs)
    cross_part(out, rows, starts, gain, order, mine, near * head_dim, row * group * length, result, head_dim)


def near_kernel(dims, axis, delta, count, order, windows, q, kv, *refs):
    group, slots, near, head_dim, block = dims
    device = lax.axis_index(axis)
    row = device // group
    mine = lax.rem(device, group) * slots
    length = q.shape[1]
    parts = group * length // block
    if delta == 2:
        state, peak, total, acc = refs
    else:
        sums, stats_out, peak, total, acc = refs

    spans = [windows[order[mine + head]] for head in range(near)]

    def pick(start, size, column):
        return q[pl.ds(start, size), :, column]

    def one(part, carry):
        span = pl.ds(pl.multiple_of(part * block, block), block)
        reset(peak, total, acc)
        limit = jnp.where(row + delta < count, 2 * WIN, -1) if delta > 0 else 2 * WIN
        attend(kv, pick, spans, part, delta * parts, limit, parts, (peak, total, acc), block, head_dim)
        for head in range(near):
            if delta == 2:
                write_state(state, head, span, peak[head, 0:1, :], total[head, 0:1, :], acc[head], head_dim)
            else:
                sums[head, :, span] = acc[head]
                stats_out[head, 0:1, span] = peak[head, 0:1, :]
                stats_out[head, 1:2, span] = total[head, 0:1, :]
        return carry

    lax.fori_loop(0, parts, one, 0)


def write_state(state, head, span, peak, total, acc, head_dim):
    state[head, 0:head_dim, span] = acc.astype(BF16)
    width = peak.shape[1]
    index = lax.broadcasted_iota(jnp.int32, (16, width), 0)
    stats = jnp.zeros((16, width), F32)
    for k, piece in enumerate(pieces(peak) + pieces(total)):
        stats = jnp.where(index == k, piece.astype(F32), stats)
    state[head, head_dim : head_dim + 16, span] = stats.astype(BF16)


def merged_state(state, sums, stats, head, span, valid, head_dim):
    factor = math.log2(math.e) / math.sqrt(head_dim)
    arrived = state[head, head_dim : head_dim + 16, span].astype(F32)
    far_peak = jnp.where(valid, arrived[0:1] + arrived[1:2] + arrived[2:3], FLOOR)
    far_total = jnp.where(valid, arrived[3:4] + arrived[4:5] + arrived[5:6], 0.0)
    peak, total = stats[head, 0:1, span], stats[head, 1:2, span]
    high = jnp.maximum(peak, far_peak)
    here = jnp.exp2((peak - high) * factor)
    there = jnp.where(valid, jnp.exp2((far_peak - high) * factor), 0.0)
    acc = sums[head, :, span] * here
    arrived_sum = jnp.where(valid, state[head, 0:head_dim, span].astype(F32), 0.0)
    return high, total * here + far_total * there, acc + arrived_sum * there


def merge_kernel(dims, axis, arrived, sums, stats, state):
    group, _, near, head_dim, block = dims
    valid = lax.axis_index(axis) // group >= 1
    width = sums.shape[2]

    def one(index, carry):
        head = index // (width // block)
        span = pl.ds(pl.multiple_of(lax.rem(index, width // block) * block, block), block)
        peak, total, acc = merged_state(arrived, sums, stats, head, span, valid, head_dim)
        write_state(state, head, span, peak, total, acc, head_dim)
        return carry

    lax.fori_loop(0, near * (width // block), one, 0)


def last_kernel(dims, axis, order, arrived, sums, stats, rows, starts, gain, other, *refs):
    group, slots, near, head_dim, block = dims
    outs, (result, out) = refs[:group], refs[group:]
    row = lax.axis_index(axis) // group
    mine = lax.rem(lax.axis_index(axis), group) * slots
    length = out.shape[1]
    parts = group * length // block
    shards = block // length

    def one(index, carry):
        head = index // parts
        part = lax.rem(index, parts)
        span = pl.ds(pl.multiple_of(part * block, block), block)
        _, total, acc = merged_state(arrived, sums, stats, head, span, row >= 1, head_dim)
        done = (acc / total).astype(BF16).T
        out[pl.ds(part * shards, shards), :, lanes(head, head_dim)] = done.reshape(shards, length, head_dim)
        return carry

    lax.fori_loop(0, parts * near, one, 0)
    scatter_blocks(axis, out, outs)
    width = other.shape[2]
    result[:, :, 0:width] = other[...]
    cross_part(
        out, rows, starts, gain, order, mine, 0, row * group * length, result, head_dim, base=width
    )


def finish_kernel(dims, axis, order, cross, cont, *refs):
    group, slots, near, head_dim = dims
    far_out, near_out, (self_out, cross_out) = refs[:group], refs[group : 2 * group], refs[2 * group :]
    mine = lax.rem(lax.axis_index(axis), group)
    far = slots - near
    for k in range(group):
        first = jnp.bitwise_xor(mine, k) * slots
        for slot in range(slots):
            source, c = (near_out, slot) if slot < near else (far_out, slot - near)
            self_out[:, lanes(order[first + slot], head_dim)] = source[k][:, c * head_dim : (c + 1) * head_dim]
    factor = math.log2(math.e) / math.sqrt(head_dim)
    clen = cont.shape[1]
    row_index = lax.broadcasted_iota(jnp.int32, (clen, clen), 0)
    key_index = lax.broadcasted_iota(jnp.int32, (clen, clen), 1)
    visible = (key_index <= row_index) & (key_index // CLEN == row_index // CLEN)
    for g in range(group):
        for slot in range(slots):
            column = lanes(order[g * slots + slot], head_dim)
            base, c, heads = ((far + 1) * head_dim, slot, near) if slot < near else (0, slot - near, far)
            tail = base + heads * head_dim
            stats = cross[:, g, :, tail : tail + head_dim].astype(F32)
            k = 6 * c
            high = stats[:, :, k : k + 1] + stats[:, :, k + 1 : k + 2] + stats[:, :, k + 2 : k + 3]
            total = stats[:, :, k + 3 : k + 4] + stats[:, :, k + 4 : k + 5] + stats[:, :, k + 5 : k + 6]
            scores = jnp.where(visible, dot(cont[0, :, column], cont[1, :, column], (1, 1)), NEGATIVE)
            final = jnp.maximum(jnp.max(high, axis=0), jnp.max(scores, axis=1, keepdims=True))
            weight = jnp.exp2((high - final[None]) * factor)
            expo = jnp.exp2((scores - final) * factor)
            own = dot(expo.astype(BF16), cont[2, :, column], (1, 0))
            denominator = jnp.sum(weight * total, axis=0) + jnp.sum(expo, axis=1, keepdims=True)
            summed = cross[:, g, :, base + c * head_dim : base + (c + 1) * head_dim].astype(F32) * weight
            merged = jnp.sum(summed, axis=0) + own
            cross_out[:, column] = (merged / denominator).astype(BF16)


def per_device(self_qkv, windows, k_gain, cont_qkv, starts):
    axis = "ctx"
    length, features = self_qkv.shape[1:]
    head_count = windows.shape[0]
    head_dim = features // head_count
    devices = lax.axis_size(axis)
    group = WIN // (2 * length)
    slots = head_count // group
    near = slots // 2
    far = slots - near
    count = devices // group
    block = 2 * length
    rows_here = cont_qkv.shape[1]
    rows_all = rows_here * devices
    nearby, distant = near * head_dim, far * head_dim
    dims = (group, slots, near, head_dim)
    big = dims + (block,)
    index = jnp.arange(head_count, dtype=jnp.int32)
    above = (windows[None, :] > windows[:, None]) | (
        (windows[None, :] == windows[:, None]) & (index[None, :] < index[:, None])
    )
    rank = jnp.sum(above.astype(jnp.int32), axis=1)
    place = lax.rem(rank, group) * slots + rank // group
    order = jnp.sum(jnp.where(place[None, :] == index[:, None], index[None, :], 0), axis=1)

    def exchange(blocks):
        got = [blocks[0]]
        for k in range(1, group):
            got.append(lax.ppermute(blocks[k], axis, [(source, source ^ k) for source in range(devices)]))
        return got

    def gather(blocks, micros):
        return pl.pallas_call(
            functools.partial(gather_kernel, axis),
            out_shape=jax.ShapeDtypeStruct((group,) + blocks[0].shape, BF16),
            in_specs=[ANY] * group,
            out_specs=VMEM,
            scratch_shapes=[pltpu.SemaphoreType.DMA((group,))],
            cost_estimate=cost(micros),
        )(*blocks)

    def up(value):
        return lax.ppermute(value, axis, [(k, k + group) for k in range(devices - group)])

    def down(value):
        return lax.ppermute(value, axis, [(k + group, k) for k in range(devices - group)])

    def call(kernel, micros, shapes, *operands, smem=2, **more):
        return pl.pallas_call(
            kernel,
            out_shape=shapes,
            in_specs=[SMEM] * smem + [VMEM] * (len(operands) - smem),
            out_specs=jax.tree.map(lambda _: VMEM, shapes),
            cost_estimate=cost(micros),
            **more,
        )(*operands)

    def shape(*sizes, dtype=BF16):
        return jax.ShapeDtypeStruct(sizes, dtype)

    packed = pl.pallas_call(
        functools.partial(pack_kernel, dims, axis),
        grid=(3, 2),
        out_shape=(shape(2, length, distant),) * group
        + (shape(length, nearby),) * group
        + (shape(3, length, nearby),) * group,
        in_specs=[SMEM, pl.BlockSpec((1, length // 2, features), lambda i, j: (lax.rem(i + 1, 3), j, 0))],
        out_specs=(
            pl.BlockSpec(
                (1, length // 2, distant), lambda i, j: (jnp.minimum(i, 1), jnp.where(i < 2, j, 1), 0)
            ),
        )
        * group
        + (pl.BlockSpec((length // 2, nearby), lambda i, j: (jnp.where(i < 2, 0, j), 0)),) * group
        + (pl.BlockSpec((1, length // 2, nearby), lambda i, j: (i, j, 0)),) * group,
        name="pack",
        cost_estimate=cost(4),
    )(order, self_qkv)
    q_near0 = gather(exchange(packed[group : 2 * group]), 1)
    kv_far0 = gather(exchange(packed[:group]), 2)
    rest0 = gather(exchange(packed[2 * group :]), 2)
    rows_sent = call(
        functools.partial(pack_rows_kernel, dims), 2, shape(devices, rows_here, slots * head_dim), order,
        cont_qkv, smem=1,
    )
    rows = lax.all_to_all(rows_sent, axis, 0, 0, tiled=True)
    row_starts = jnp.broadcast_to(starts[:, None], (starts.shape[0], rows_all // starts.shape[0])).reshape(rows_all, 1)
    gain = k_gain.reshape(head_count, head_dim)

    kv_far1 = up(kv_far0)
    q_near1 = down(q_near0)
    half = group // 2
    kv_far2 = up(kv_far1[half:])
    deep = jnp.sum((windows > (group + group - half) * length + 1).astype(jnp.int32)) > group * near
    kv_far3 = lax.cond(deep, lambda value: up(value), lambda value: value, kv_far1[:half])
    q_near2 = down(q_near1)

    state_scratch = [
        pltpu.VMEM((far, 8, block), F32),
        pltpu.VMEM((far, 8, block), F32),
        pltpu.VMEM((far, head_dim, block), F32),
    ]
    state_shape = shape(near, head_dim + 16, group * length)
    local_shape = (shape(near, head_dim, group * length, dtype=F32), shape(near, 8, group * length, dtype=F32))

    def near_step(delta, q):
        return call(
            functools.partial(near_kernel, big, axis, delta, count), 7,
            state_shape if delta == 2 else local_shape, order, windows, q, rest0, scratch_shapes=state_scratch,
        )

    def merge(kernel, micros, shapes, *operands, **more):
        return call(functools.partial(kernel, big, axis), micros, shapes, *operands, **more)

    state2 = up(near_step(2, q_near2))
    state1 = up(merge(merge_kernel, 1, state_shape, state2, *near_step(1, q_near1), smem=0))
    local0 = near_step(0, q_near0)

    *far_out, far_cross = pl.pallas_call(
        functools.partial(far_kernel, big, axis),
        out_shape=(shape(length, distant),) * group + (shape(devices, rows_here, distant + head_dim),),
        in_specs=[SMEM, SMEM, VMEM, ANY, ANY, ANY, ANY, VMEM, VMEM, VMEM],
        out_specs=(VMEM,) * (group + 1),
        scratch_shapes=[pltpu.VMEM((group, length, distant), BF16), pltpu.VMEM((3 * group, 2, length, distant), BF16)]
        + state_scratch
        + [pltpu.SemaphoreType.DMA((4,))],
        name="far",
        cost_estimate=cost(14),
    )(order, windows, rest0, kv_far0, kv_far1, kv_far2, kv_far3, rows, row_starts, gain)
    far_back = exchange(far_out)
    *near_out, cross = merge(
        last_kernel, 4,
        (shape(length, nearby),) * group + (shape(devices, rows_here, distant + nearby + 2 * head_dim),),
        order, state1, *local0, rows, row_starts, gain, far_cross, smem=1,
        scratch_shapes=[pltpu.VMEM((group, length, nearby), BF16)],
    )
    near_back = exchange(near_out)
    cross = lax.all_to_all(cross, axis, 0, 0, tiled=True)
    cross = cross.reshape((count, group) + cross.shape[1:])
    return call(
        functools.partial(finish_kernel, dims, axis), 4, (shape(length, features), shape(rows_here, features)),
        order, cross, cont_qkv, *far_back, *near_back, smem=1,
    )


def solution(mesh):
    in_specs = (
        P(None, ("groups", "ctx"), None),
        P(),
        P(),
        P(None, ("groups", "ctx"), None),
        P("groups"),
    )
    out_specs = (P(("groups", "ctx"), None), P(("groups", "ctx"), None))

    return jax.shard_map(per_device, mesh=mesh, in_specs=in_specs, out_specs=out_specs, check_vma=False)
```

```python
import functools
import math

import jax
import jax.numpy as jnp
from jax import lax
from jax.experimental import pallas as pl
from jax.experimental.pallas import tpu as pltpu
from jax.sharding import PartitionSpec as P


WIN = 2048
CLEN = 8

EPSILON = 1e-06
NEGATIVE = -1e30
FLOOR = -1e29
BF16 = jnp.bfloat16
F32 = jnp.float32

SMEM = pl.BlockSpec(memory_space=pltpu.SMEM)
VMEM = pl.BlockSpec(memory_space=pltpu.VMEM)
ANY = pl.BlockSpec(memory_space=pl.ANY)


GRANT = pltpu.CompilerParams(vmem_limit_bytes=20 * 2**20)


def cost(micros):
    return pl.CostEstimate(flops=int(micros * 1.15e9), bytes_accessed=0, transcendentals=0)


def pieces(value):
    high = value.astype(BF16)
    rest = value - high.astype(F32)
    middle = rest.astype(BF16)
    low = (rest - middle.astype(F32)).astype(BF16)
    return high, middle, low


def dot(left, right, contract):
    return lax.dot_general(left, right, ((contract[:1], contract[1:]), ((), ())), preferred_element_type=F32)


def lanes(head, head_dim):
    return pl.ds(pl.multiple_of(head * head_dim, head_dim), head_dim)


def pack_kernel(dims, axis, order, qkv, *outs):
    group, slots, near, head_dim = dims
    step = pl.program_id(0)
    far = slots - near
    mine = lax.rem(lax.axis_index(axis), group)
    for k in range(group):
        kv_far, q_near, rest = outs[k], outs[group + k], outs[2 * group + k]
        first = jnp.bitwise_xor(mine, k) * slots

        def move(target, spot, start, heads):
            for c in range(heads):
                column = slice(c * head_dim, (c + 1) * head_dim)
                target[spot + (slice(None), column)] = qkv[0, :, lanes(order[start + c], head_dim)]

        @pl.when(step == 2)
        def _():
            move(q_near, (), first, near)
            move(rest, (0,), first + near, far)

        @pl.when(step < 2)
        def _():
            move(rest, (0,), first, near)
            move(kv_far, (0,), first + near, far)


def gather_kernel(axis, *refs):
    group = len(refs) - 2
    blocks, out, sems = refs[:group], refs[group], refs[group + 1]
    mine = lax.rem(lax.axis_index(axis), group)
    copies = [
        pltpu.make_async_copy(block, out.at[jnp.bitwise_xor(mine, k)], sems.at[k]) for k, block in enumerate(blocks)
    ]
    for copy in copies:
        copy.start()
    for copy in copies:
        copy.wait()


def pack_rows_kernel(dims, order, rows, out):
    group, slots, _, head_dim = dims
    for device in range(out.shape[0]):
        for c in range(slots):
            out[device, :, c * head_dim : (c + 1) * head_dim] = rows[
                0, :, lanes(order[(device % group) * slots + c], head_dim)
            ]


def attend(kv, queries, windows, part, base, high_limit, key_parts, state, block, head_dim):
    peak, total, acc = state
    shards = block // kv.shape[2]
    factor = math.log2(math.e) / math.sqrt(head_dim)
    row_index = lax.broadcasted_iota(jnp.int32, (block, block), 1)
    key_index = lax.broadcasted_iota(jnp.int32, (block, block), 0)

    def step(distance, diagonal, heads):
        spot = pl.ds((base + part - distance) * shards, shards)
        for head in range(heads):
            window = windows[head]
            column = slice(head * head_dim, (head + 1) * head_dim)
            keys = kv[spot, 0, :, column].reshape(block, head_dim)
            values = kv[spot, 1, :, column].reshape(block, head_dim)
            q = queries(part * shards, shards, column).reshape(block, head_dim)
            scores = dot(keys, q, (1, 1))
            visible = row_index < key_index + (window - distance * block)
            if diagonal:
                visible = visible & (row_index >= key_index)
            scores = jnp.where(visible, scores, NEGATIVE)
            old = peak[head, 0:1, :]
            new = jnp.maximum(old, jnp.max(scores, axis=0, keepdims=True))
            fade = jnp.exp2((old - new) * factor)
            expo = jnp.exp2((scores - new) * factor)
            total[head, 0:1, :] = total[head, 0:1, :] * fade + jnp.sum(expo, axis=0, keepdims=True)
            peak[head, 0:1, :] = new
            acc[head] = acc[head] * fade + dot(values, expo.astype(BF16), (0, 0))

    limit = jnp.minimum(base + part, high_limit)
    ends = [jnp.minimum((window + block - 2) // block, limit) + 1 for window in windows]
    low = jnp.maximum(base + part - (key_parts - 1), 0)

    if base - (key_parts - 1) <= 0:

        @pl.when(low == 0)
        def _():
            step(0, True, len(windows))

    start = jnp.maximum(low, 1)
    for heads in range(len(windows), 0, -1):

        def loop(distance, carry, heads=heads):
            step(distance, False, heads)
            return carry

        lax.fori_loop(start, ends[heads - 1], loop, 0)
        start = jnp.maximum(start, ends[heads - 1])


def cross_part(out, rows, starts, gain, order, first, offset, anchor, result, head_dim, base=0):
    heads = out.shape[2] // head_dim
    keys_here = out.shape[0] * out.shape[1]
    clen = rows.shape[1]
    devices = rows.shape[0]
    block = min(devices * clen, 128)
    per = block // clen
    factor = math.log2(math.e) / math.sqrt(head_dim)
    tail = slice(base + heads * head_dim, base + (heads + 1) * head_dim)
    for c in range(heads):
        column = slice(c * head_dim, (c + 1) * head_dim)
        values = out[:, :, column].reshape(keys_here, head_dim)
        hidden = values.astype(F32)
        norm = hidden * lax.rsqrt(jnp.mean(hidden * hidden, axis=-1, keepdims=True) + EPSILON)
        keys = (norm * gain[pl.ds(order[first + c], 1), :]).astype(BF16)

        def blocks(index, carry):
            spot = pl.ds(index * per, per)
            q = rows[spot, :, offset + c * head_dim : offset + (c + 1) * head_dim].reshape(block, head_dim)
            scores = dot(q, keys, (1, 1))
            position = anchor + lax.broadcasted_iota(jnp.int32, (block, keys_here), 1)
            which = lax.broadcasted_iota(jnp.int32, (block, 1), 0) // CLEN
            limits = jnp.zeros((block, 1), jnp.int32)
            for k in range(block // CLEN):
                limits = jnp.where(which == k, starts[index * (block // CLEN) + k], limits)
            seen = position < limits
            scores = jnp.where(seen, scores, NEGATIVE)
            high = jnp.maximum(jnp.max(scores, axis=1, keepdims=True), FLOOR)
            expo = jnp.exp2((scores - high) * factor)
            total = jnp.sum(expo, axis=1, keepdims=True)
            summed = dot(expo.astype(BF16), values, (1, 0))
            result[spot, :, base + c * head_dim : base + (c + 1) * head_dim] = summed.astype(BF16).reshape(
                per, clen, head_dim
            )
            lane = lax.broadcasted_iota(jnp.int32, (block, head_dim), 1)
            stats = jnp.zeros((block, head_dim), F32) if c == 0 else None
            for k, piece in enumerate(pieces(high) + pieces(total)):
                value = jnp.broadcast_to(piece.astype(F32), (block, head_dim))
                if stats is None:
                    stats = result[spot, :, tail].reshape(block, head_dim).astype(F32)
                stats = jnp.where(lane == c * 6 + k, value, stats)
            result[spot, :, tail] = stats.astype(BF16).reshape(per, clen, head_dim)
            return carry

        lax.fori_loop(0, devices * clen // block, blocks, 0)


def scatter_blocks(axis, value, outs):
    mine = lax.rem(lax.axis_index(axis), len(outs))
    for k, out in enumerate(outs):
        out[...] = value[jnp.bitwise_xor(mine, k)]


def reset(peak, total, acc):
    peak[...] = jnp.full(peak.shape, FLOOR, F32)
    total[...] = jnp.zeros(total.shape, F32)
    acc[...] = jnp.zeros(acc.shape, F32)


def far_kernel(dims, axis, order, windows, rest, kv0, kv1, kv2, kv3, rows, starts, gain, *refs):
    group, slots, near, head_dim, block = dims
    outs, (result, out, kv, peak, total, acc, sems) = refs[:group], refs[group:]
    device = lax.axis_index(axis)
    row = device // group
    mine = lax.rem(device, group) * slots + near
    copies, start = [], 0
    for k, source in enumerate((kv3, kv2, kv1, kv0)):
        copies.append(pltpu.make_async_copy(source, kv.at[pl.ds(start, source.shape[0])], sems.at[k]))
        start += source.shape[0]
    for copy in copies[::-1]:
        copy.start()
    for copy in copies[::-1]:
        copy.wait()
    length = out.shape[1]
    parts = group * length // block
    shards = block // length

    heads = slots - near
    spans = [windows[order[mine + head]] for head in range(heads)]

    def pick(start, size, column):
        return rest[pl.ds(start, size), 2, :, column]

    def one(part, carry):
        reset(peak, total, acc)
        attend(kv, pick, spans, part, 2 * parts, row * parts + part, 3 * parts, (peak, total, acc), block, head_dim)
        for head in range(heads):
            done = (acc[head] / total[head, 0:1, :]).astype(BF16).T
            column = slice(head * head_dim, (head + 1) * head_dim)
            out[pl.ds(part * shards, shards), :, column] = done.reshape(shards, length, head_dim)
        return carry

    lax.fori_loop(0, parts, one, 0)
    scatter_blocks(axis, out, outs)
    cross_part(out, rows, starts, gain, order, mine, near * head_dim, row * group * length, result, head_dim)


def near_kernel(dims, axis, delta, count, order, windows, q, kv, *refs):
    group, slots, near, head_dim, block = dims
    device = lax.axis_index(axis)
    row = device // group
    mine = lax.rem(device, group) * slots
    length = q.shape[1]
    parts = group * length // block
    if delta == 2:
        state, peak, total, acc = refs
    else:
        sums, stats_out, peak, total, acc = refs

    spans = [windows[order[mine + head]] for head in range(near)]

    def pick(start, size, column):
        return q[pl.ds(start, size), :, column]

    def one(part, carry):
        span = pl.ds(pl.multiple_of(part * block, block), block)
        reset(peak, total, acc)
        limit = jnp.where(row + delta < count, 2 * WIN, -1) if delta > 0 else 2 * WIN
        attend(kv, pick, spans, part, delta * parts, limit, parts, (peak, total, acc), block, head_dim)
        for head in range(near):
            if delta == 2:
                write_state(state, head, span, peak[head, 0:1, :], total[head, 0:1, :], acc[head], head_dim)
            else:
                sums[head, :, span] = acc[head]
                stats_out[head, 0:1, span] = peak[head, 0:1, :]
                stats_out[head, 1:2, span] = total[head, 0:1, :]
        return carry

    lax.fori_loop(0, parts, one, 0)


def write_state(state, head, span, peak, total, acc, head_dim):
    state[head, 0:head_dim, span] = acc.astype(BF16)
    width = peak.shape[1]
    index = lax.broadcasted_iota(jnp.int32, (16, width), 0)
    stats = jnp.zeros((16, width), F32)
    for k, piece in enumerate(pieces(peak) + pieces(total)):
        stats = jnp.where(index == k, piece.astype(F32), stats)
    state[head, head_dim : head_dim + 16, span] = stats.astype(BF16)


def merged_state(state, sums, stats, head, span, valid, head_dim):
    factor = math.log2(math.e) / math.sqrt(head_dim)
    arrived = state[head, head_dim : head_dim + 16, span].astype(F32)
    far_peak = jnp.where(valid, arrived[0:1] + arrived[1:2] + arrived[2:3], FLOOR)
    far_total = jnp.where(valid, arrived[3:4] + arrived[4:5] + arrived[5:6], 0.0)
    peak, total = stats[head, 0:1, span], stats[head, 1:2, span]
    high = jnp.maximum(peak, far_peak)
    here = jnp.exp2((peak - high) * factor)
    there = jnp.where(valid, jnp.exp2((far_peak - high) * factor), 0.0)
    acc = sums[head, :, span] * here
    arrived_sum = jnp.where(valid, state[head, 0:head_dim, span].astype(F32), 0.0)
    return high, total * here + far_total * there, acc + arrived_sum * there


def merge_kernel(dims, axis, arrived, sums, stats, state):
    group, _, near, head_dim, block = dims
    valid = lax.axis_index(axis) // group >= 1
    width = sums.shape[2]

    def one(index, carry):
        head = index // (width // block)
        span = pl.ds(pl.multiple_of(lax.rem(index, width // block) * block, block), block)
        peak, total, acc = merged_state(arrived, sums, stats, head, span, valid, head_dim)
        write_state(state, head, span, peak, total, acc, head_dim)
        return carry

    lax.fori_loop(0, near * (width // block), one, 0)


def last_kernel(dims, axis, order, starts, arrived, sums, stats, rows, gain, other, *refs):
    group, slots, near, head_dim, block = dims
    outs, (result, out) = refs[:group], refs[group:]
    row = lax.axis_index(axis) // group
    mine = lax.rem(lax.axis_index(axis), group) * slots
    length = out.shape[1]
    parts = group * length // block
    shards = block // length

    def one(index, carry):
        head = index // parts
        part = lax.rem(index, parts)
        span = pl.ds(pl.multiple_of(part * block, block), block)
        _, total, acc = merged_state(arrived, sums, stats, head, span, row >= 1, head_dim)
        done = (acc / total).astype(BF16).T
        out[pl.ds(part * shards, shards), :, lanes(head, head_dim)] = done.reshape(shards, length, head_dim)
        return carry

    lax.fori_loop(0, parts * near, one, 0)
    scatter_blocks(axis, out, outs)
    width = other.shape[2]
    result[:, :, 0:width] = other[...]
    cross_part(
        out, rows, starts, gain, order, mine, 0, row * group * length, result, head_dim, base=width
    )


def finish_kernel(dims, axis, order, cross, cont, *refs):
    group, slots, near, head_dim = dims
    far_out, near_out, (self_out, cross_out) = refs[:group], refs[group : 2 * group], refs[2 * group :]
    mine = lax.rem(lax.axis_index(axis), group)
    far = slots - near
    for k in range(group):
        first = jnp.bitwise_xor(mine, k) * slots
        for slot in range(slots):
            source, c = (near_out, slot) if slot < near else (far_out, slot - near)
            self_out[:, lanes(order[first + slot], head_dim)] = source[k][:, c * head_dim : (c + 1) * head_dim]
    factor = math.log2(math.e) / math.sqrt(head_dim)
    clen = cont.shape[1]
    row_index = lax.broadcasted_iota(jnp.int32, (clen, clen), 0)
    key_index = lax.broadcasted_iota(jnp.int32, (clen, clen), 1)
    visible = (key_index <= row_index) & (key_index // CLEN == row_index // CLEN)
    for g in range(group):
        for slot in range(slots):
            column = lanes(order[g * slots + slot], head_dim)
            base, c, heads = ((far + 1) * head_dim, slot, near) if slot < near else (0, slot - near, far)
            tail = base + heads * head_dim
            stats = cross[:, g, :, tail : tail + head_dim].astype(F32)
            k = 6 * c
            high = stats[:, :, k : k + 1] + stats[:, :, k + 1 : k + 2] + stats[:, :, k + 2 : k + 3]
            total = stats[:, :, k + 3 : k + 4] + stats[:, :, k + 4 : k + 5] + stats[:, :, k + 5 : k + 6]
            scores = jnp.where(visible, dot(cont[0, :, column], cont[1, :, column], (1, 1)), NEGATIVE)
            final = jnp.maximum(jnp.max(high, axis=0), jnp.max(scores, axis=1, keepdims=True))
            weight = jnp.exp2((high - final[None]) * factor)
            expo = jnp.exp2((scores - final) * factor)
            own = dot(expo.astype(BF16), cont[2, :, column], (1, 0))
            denominator = jnp.sum(weight * total, axis=0) + jnp.sum(expo, axis=1, keepdims=True)
            summed = cross[:, g, :, base + c * head_dim : base + (c + 1) * head_dim].astype(F32) * weight
            merged = jnp.sum(summed, axis=0) + own
            cross_out[:, column] = (merged / denominator).astype(BF16)


def per_device(self_qkv, windows, k_gain, cont_qkv, starts):
    axis = "ctx"
    length, features = self_qkv.shape[1:]
    head_count = windows.shape[0]
    head_dim = features // head_count
    devices = lax.axis_size(axis)
    group = WIN // (2 * length)
    slots = head_count // group
    near = slots // 2
    far = slots - near
    count = devices // group
    block = 2 * length
    rows_here = cont_qkv.shape[1]
    nearby, distant = near * head_dim, far * head_dim
    dims = (group, slots, near, head_dim)
    big = dims + (block,)
    index = jnp.arange(head_count, dtype=jnp.int32)
    above = (windows[None, :] > windows[:, None]) | (
        (windows[None, :] == windows[:, None]) & (index[None, :] < index[:, None])
    )
    rank = jnp.sum(above.astype(jnp.int32), axis=1)
    place = lax.rem(rank, group) * slots + rank // group
    order = jnp.sum(jnp.where(place[None, :] == index[:, None], index[None, :], 0), axis=1)

    def exchange(blocks):
        got = [blocks[0]]
        for k in range(1, group):
            got.append(lax.ppermute(blocks[k], axis, [(source, source ^ k) for source in range(devices)]))
        return got

    def gather(blocks, micros):
        return pl.pallas_call(
            functools.partial(gather_kernel, axis),
            out_shape=jax.ShapeDtypeStruct((group,) + blocks[0].shape, BF16),
            in_specs=[ANY] * group,
            out_specs=VMEM,
            scratch_shapes=[pltpu.SemaphoreType.DMA((group,))],
            cost_estimate=cost(micros),
        compiler_params=GRANT,
        )(*blocks)

    def up(value):
        return lax.ppermute(value, axis, [(k, k + group) for k in range(devices - group)])

    def down(value):
        return lax.ppermute(value, axis, [(k + group, k) for k in range(devices - group)])

    def call(kernel, micros, shapes, *operands, smem=2, **more):
        return pl.pallas_call(
            kernel,
            out_shape=shapes,
            in_specs=[SMEM] * smem + [VMEM] * (len(operands) - smem),
            out_specs=jax.tree.map(lambda _: VMEM, shapes),
            cost_estimate=cost(micros),
        compiler_params=GRANT,
            **more,
        )(*operands)

    def shape(*sizes, dtype=BF16):
        return jax.ShapeDtypeStruct(sizes, dtype)

    packed = pl.pallas_call(
        functools.partial(pack_kernel, dims, axis),
        grid=(3, 2),
        out_shape=(shape(2, length, distant),) * group
        + (shape(length, nearby),) * group
        + (shape(3, length, nearby),) * group,
        in_specs=[SMEM, pl.BlockSpec((1, length // 2, features), lambda i, j: (lax.rem(i + 1, 3), j, 0))],
        out_specs=(
            pl.BlockSpec(
                (1, length // 2, distant), lambda i, j: (jnp.minimum(i, 1), jnp.where(i < 2, j, 1), 0)
            ),
        )
        * group
        + (pl.BlockSpec((length // 2, nearby), lambda i, j: (jnp.where(i < 2, 0, j), 0)),) * group
        + (pl.BlockSpec((1, length // 2, nearby), lambda i, j: (i, j, 0)),) * group,
        name="pack",
        cost_estimate=cost(4),
        compiler_params=GRANT,
    )(order, self_qkv)
    q_near0 = gather(exchange(packed[group : 2 * group]), 1)
    kv_far0 = gather(exchange(packed[:group]), 2)
    rest0 = gather(exchange(packed[2 * group :]), 2)
    rows_sent = call(
        functools.partial(pack_rows_kernel, dims), 2, shape(devices, rows_here, slots * head_dim), order,
        cont_qkv, smem=1,
    )
    rows = lax.all_to_all(rows_sent, axis, 0, 0, tiled=True)
    gain = k_gain.reshape(head_count, head_dim)

    kv_far1 = up(kv_far0)
    q_near1 = down(q_near0)
    half = group // 2
    kv_far2 = up(kv_far1[half:])
    deep = jnp.sum((windows > (group + group - half) * length + 1).astype(jnp.int32)) > group * near
    kv_far3 = lax.cond(deep, lambda value: up(value), lambda value: value, kv_far1[:half])
    q_near2 = down(q_near1)

    state_scratch = [
        pltpu.VMEM((far, 8, block), F32),
        pltpu.VMEM((far, 8, block), F32),
        pltpu.VMEM((far, head_dim, block), F32),
    ]
    state_shape = shape(near, head_dim + 16, group * length)
    local_shape = (shape(near, head_dim, group * length, dtype=F32), shape(near, 8, group * length, dtype=F32))

    def near_step(delta, q):
        return call(
            functools.partial(near_kernel, big, axis, delta, count), 7,
            state_shape if delta == 2 else local_shape, order, windows, q, rest0, scratch_shapes=state_scratch,
        )

    def merge(kernel, micros, shapes, *operands, **more):
        return call(functools.partial(kernel, big, axis), micros, shapes, *operands, **more)

    state2 = up(near_step(2, q_near2))
    state1 = up(merge(merge_kernel, 1, state_shape, state2, *near_step(1, q_near1), smem=0))
    local0 = near_step(0, q_near0)

    *far_out, far_cross = pl.pallas_call(
        functools.partial(far_kernel, big, axis),
        out_shape=(shape(length, distant),) * group + (shape(devices, rows_here, distant + head_dim),),
        in_specs=[SMEM, SMEM, VMEM, ANY, ANY, ANY, ANY, VMEM, SMEM, VMEM],
        out_specs=(VMEM,) * (group + 1),
        scratch_shapes=[pltpu.VMEM((group, length, distant), BF16), pltpu.VMEM((3 * group, 2, length, distant), BF16)]
        + state_scratch
        + [pltpu.SemaphoreType.DMA((4,))],
        name="far",
        cost_estimate=cost(14),
        compiler_params=GRANT,
    )(order, windows, rest0, kv_far0, kv_far1, kv_far2, kv_far3, rows, starts, gain)
    far_back = exchange(far_out)
    *near_out, cross = merge(
        last_kernel, 4,
        (shape(length, nearby),) * group + (shape(devices, rows_here, distant + nearby + 2 * head_dim),),
        order, starts, state1, *local0, rows, gain, far_cross, smem=2,
        scratch_shapes=[pltpu.VMEM((group, length, nearby), BF16)],
    )
    near_back = exchange(near_out)
    cross = lax.all_to_all(cross, axis, 0, 0, tiled=True)
    cross = cross.reshape((count, group) + cross.shape[1:])
    return call(
        functools.partial(finish_kernel, dims, axis), 4, (shape(length, features), shape(rows_here, features)),
        order, cross, cont_qkv, *far_back, *near_back, smem=1,
    )


def solution(mesh):
    in_specs = (
        P(None, ("groups", "ctx"), None),
        P(),
        P(),
        P(None, ("groups", "ctx"), None),
        P("groups"),
    )
    out_specs = (P(("groups", "ctx"), None), P(("groups", "ctx"), None))

    return jax.shard_map(per_device, mesh=mesh, in_specs=in_specs, out_specs=out_specs, check_vma=False)
```

```python
import functools
import math

import jax
import jax.numpy as jnp
from jax import lax
from jax.experimental import pallas as pl
from jax.experimental.pallas import tpu as pltpu
from jax.sharding import PartitionSpec as P


WIN = 2048
CLEN = 8

EPSILON = 1e-06
NEGATIVE = -1e30
FLOOR = -1e29
BF16 = jnp.bfloat16
F32 = jnp.float32

SMEM = pl.BlockSpec(memory_space=pltpu.SMEM)
VMEM = pl.BlockSpec(memory_space=pltpu.VMEM)
ANY = pl.BlockSpec(memory_space=pl.ANY)


GRANT = pltpu.CompilerParams(vmem_limit_bytes=20 * 2**20)


def cost(micros):
    return pl.CostEstimate(flops=int(micros * 1.15e9), bytes_accessed=0, transcendentals=0)


def pieces(value):
    high = value.astype(BF16)
    rest = value - high.astype(F32)
    middle = rest.astype(BF16)
    low = (rest - middle.astype(F32)).astype(BF16)
    return high, middle, low


def dot(left, right, contract):
    return lax.dot_general(left, right, ((contract[:1], contract[1:]), ((), ())), preferred_element_type=F32)


def lanes(head, head_dim):
    return pl.ds(pl.multiple_of(head * head_dim, head_dim), head_dim)


def pack_kernel(dims, axis, order, qkv, *outs):
    group, slots, near, head_dim = dims
    step = pl.program_id(0)
    far = slots - near
    mine = lax.rem(lax.axis_index(axis), group)
    for k in range(group):
        kv_far, q_near, rest = outs[k], outs[group + k], outs[2 * group + k]
        first = jnp.bitwise_xor(mine, k) * slots

        def move(target, spot, start, heads):
            for c in range(heads):
                column = slice(c * head_dim, (c + 1) * head_dim)
                target[spot + (slice(None), column)] = qkv[0, :, lanes(order[start + c], head_dim)]

        @pl.when(step == 2)
        def _():
            move(q_near, (), first, near)
            move(rest, (0,), first + near, far)

        @pl.when(step < 2)
        def _():
            move(rest, (0,), first, near)
            move(kv_far, (0,), first + near, far)


def gather_kernel(axis, *refs):
    group = len(refs) - 2
    blocks, out, sems = refs[:group], refs[group], refs[group + 1]
    mine = lax.rem(lax.axis_index(axis), group)
    copies = [
        pltpu.make_async_copy(block, out.at[jnp.bitwise_xor(mine, k)], sems.at[k]) for k, block in enumerate(blocks)
    ]
    for copy in copies:
        copy.start()
    for copy in copies:
        copy.wait()


def pack_rows_kernel(dims, order, rows, out):
    group, slots, _, head_dim = dims
    for device in range(out.shape[0]):
        for c in range(slots):
            out[device, :, c * head_dim : (c + 1) * head_dim] = rows[
                0, :, lanes(order[(device % group) * slots + c], head_dim)
            ]


def attend(kv, queries, windows, part, base, high_limit, key_parts, state, block, head_dim):
    peak, total, acc = state
    shards = block // kv.shape[2]
    factor = math.log2(math.e) / math.sqrt(head_dim)
    row_index = lax.broadcasted_iota(jnp.int32, (block, block), 1)
    key_index = lax.broadcasted_iota(jnp.int32, (block, block), 0)

    def step(distance, diagonal, heads):
        spot = pl.ds((base + part - distance) * shards, shards)
        for head in range(heads):
            window = windows[head]
            column = slice(head * head_dim, (head + 1) * head_dim)
            keys = kv[spot, 0, :, column].reshape(block, head_dim)
            values = kv[spot, 1, :, column].reshape(block, head_dim)
            q = queries(part * shards, shards, column).reshape(block, head_dim)
            scores = dot(keys, q, (1, 1))
            visible = row_index < key_index + (window - distance * block)
            if diagonal:
                visible = visible & (row_index >= key_index)
            scores = jnp.where(visible, scores, NEGATIVE)
            old = peak[head, 0:1, :]
            new = jnp.maximum(old, jnp.max(scores, axis=0, keepdims=True))
            fade = jnp.exp2((old - new) * factor)
            expo = jnp.exp2((scores - new) * factor)
            total[head, 0:1, :] = total[head, 0:1, :] * fade + jnp.sum(expo, axis=0, keepdims=True)
            peak[head, 0:1, :] = new
            acc[head] = acc[head] * fade + dot(values, expo.astype(BF16), (0, 0))

    limit = jnp.minimum(base + part, high_limit)
    ends = [jnp.minimum((window + block - 2) // block, limit) + 1 for window in windows]
    low = jnp.maximum(base + part - (key_parts - 1), 0)

    if base - (key_parts - 1) <= 0:

        @pl.when(low == 0)
        def _():
            step(0, True, len(windows))

    start = jnp.maximum(low, 1)
    for heads in range(len(windows), 0, -1):

        def loop(distance, carry, heads=heads):
            step(distance, False, heads)
            return carry

        lax.fori_loop(start, ends[heads - 1], loop, 0)
        start = jnp.maximum(start, ends[heads - 1])


def cross_part(out, rows, starts, gain, order, first, offset, anchor, result, head_dim, base=0):
    heads = out.shape[2] // head_dim
    keys_here = out.shape[0] * out.shape[1]
    clen = rows.shape[1]
    devices = rows.shape[0]
    block = min(devices * clen, 128)
    per = block // clen
    factor = math.log2(math.e) / math.sqrt(head_dim)
    tail = slice(base + heads * head_dim, base + (heads + 1) * head_dim)
    for c in range(heads):
        column = slice(c * head_dim, (c + 1) * head_dim)
        values = out[:, :, column].reshape(keys_here, head_dim)
        hidden = values.astype(F32)
        norm = hidden * lax.rsqrt(jnp.mean(hidden * hidden, axis=-1, keepdims=True) + EPSILON)
        keys = (norm * gain[pl.ds(order[first + c], 1), :]).astype(BF16)

        def blocks(index, carry):
            spot = pl.ds(index * per, per)
            q = rows[spot, :, offset + c * head_dim : offset + (c + 1) * head_dim].reshape(block, head_dim)
            scores = dot(q, keys, (1, 1))
            position = anchor + lax.broadcasted_iota(jnp.int32, (block, keys_here), 1)
            which = lax.broadcasted_iota(jnp.int32, (block, 1), 0) // CLEN
            limits = jnp.zeros((block, 1), jnp.int32)
            for k in range(block // CLEN):
                limits = jnp.where(which == k, starts[index * (block // CLEN) + k], limits)
            seen = position < limits
            scores = jnp.where(seen, scores, NEGATIVE)
            high = jnp.maximum(jnp.max(scores, axis=1, keepdims=True), FLOOR)
            expo = jnp.exp2((scores - high) * factor)
            total = jnp.sum(expo, axis=1, keepdims=True)
            summed = dot(expo.astype(BF16), values, (1, 0))
            result[spot, :, base + c * head_dim : base + (c + 1) * head_dim] = summed.astype(BF16).reshape(
                per, clen, head_dim
            )
            lane = lax.broadcasted_iota(jnp.int32, (block, head_dim), 1)
            stats = jnp.zeros((block, head_dim), F32) if c == 0 else None
            for k, piece in enumerate(pieces(high) + pieces(total)):
                value = jnp.broadcast_to(piece.astype(F32), (block, head_dim))
                if stats is None:
                    stats = result[spot, :, tail].reshape(block, head_dim).astype(F32)
                stats = jnp.where(lane == c * 6 + k, value, stats)
            result[spot, :, tail] = stats.astype(BF16).reshape(per, clen, head_dim)
            return carry

        lax.fori_loop(0, devices * clen // block, blocks, 0)


def scatter_blocks(axis, value, outs):
    mine = lax.rem(lax.axis_index(axis), len(outs))
    for k, out in enumerate(outs):
        out[...] = value[jnp.bitwise_xor(mine, k)]


def reset(peak, total, acc):
    peak[...] = jnp.full(peak.shape, FLOOR, F32)
    total[...] = jnp.zeros(total.shape, F32)
    acc[...] = jnp.zeros(acc.shape, F32)


def load(sources, kv, sems):
    copies, start = [], 0
    for k, source in enumerate(sources):
        copies.append(pltpu.make_async_copy(source, kv.at[pl.ds(start, source.shape[0])], sems.at[k]))
        start += source.shape[0]
    for copy in copies:
        copy.start()
    for copy in copies:
        copy.wait()


def far_start_kernel(dims, axis, order, windows, rest, kv0, kv1, sums, stats, kv, peak, total, acc, sems):
    group, slots, near, head_dim, block = dims
    device = lax.axis_index(axis)
    row = device // group
    mine = lax.rem(device, group) * slots + near
    load((kv1, kv0), kv, sems)
    parts = sums.shape[2] // block
    heads = slots - near
    spans = [windows[order[mine + head]] for head in range(heads)]

    def pick(start, size, column):
        return rest[pl.ds(start, size), 2, :, column]

    def one(part, carry):
        span = pl.ds(pl.multiple_of(part * block, block), block)
        reset(peak, total, acc)
        attend(kv, pick, spans, part, parts, row * parts + part, 2 * parts, (peak, total, acc), block, head_dim)
        for head in range(heads):
            sums[head, :, span] = acc[head]
            stats[head, 0:1, span] = peak[head, 0:1, :]
            stats[head, 1:2, span] = total[head, 0:1, :]
        return carry

    lax.fori_loop(0, parts, one, 0)


def far_kernel(dims, axis, order, windows, starts, rest, rows, gain, sums, stats, kv2, kv3, *refs):
    group, slots, near, head_dim, block = dims
    outs, (result, out, kv, peak, total, acc, sems) = refs[:group], refs[group:]
    device = lax.axis_index(axis)
    row = device // group
    mine = lax.rem(device, group) * slots + near
    load((kv3, kv2), kv, sems)
    length = out.shape[1]
    parts = group * length // block
    shards = block // length
    heads = slots - near
    spans = [windows[order[mine + head]] for head in range(heads)]

    def pick(start, size, column):
        return rest[pl.ds(start, size), 2, :, column]

    def one(part, carry):
        span = pl.ds(pl.multiple_of(part * block, block), block)
        for head in range(heads):
            peak[head, 0:1, :] = stats[head, 0:1, span]
            total[head, 0:1, :] = stats[head, 1:2, span]
            acc[head] = sums[head, :, span]
        attend(kv, pick, spans, part, 2 * parts, row * parts + part, parts, (peak, total, acc), block, head_dim)
        for head in range(heads):
            done = (acc[head] / total[head, 0:1, :]).astype(BF16).T
            column = slice(head * head_dim, (head + 1) * head_dim)
            out[pl.ds(part * shards, shards), :, column] = done.reshape(shards, length, head_dim)
        return carry

    lax.fori_loop(0, parts, one, 0)
    scatter_blocks(axis, out, outs)
    cross_part(out, rows, starts, gain, order, mine, near * head_dim, row * group * length, result, head_dim)


def near_kernel(dims, axis, delta, count, order, windows, q, kv, *refs):
    group, slots, near, head_dim, block = dims
    device = lax.axis_index(axis)
    row = device // group
    mine = lax.rem(device, group) * slots
    length = q.shape[1]
    parts = group * length // block
    if delta == 1:
        refs = refs[1:]
    if delta == 2:
        state, peak, total, acc = refs
    else:
        sums, stats_out, peak, total, acc = refs

    spans = [windows[order[mine + head]] for head in range(near)]

    def pick(start, size, column):
        return q[pl.ds(start, size), :, column]

    def one(part, carry):
        span = pl.ds(pl.multiple_of(part * block, block), block)
        reset(peak, total, acc)
        limit = jnp.where(row + delta < count, 2 * WIN, -1) if delta > 0 else 2 * WIN
        attend(kv, pick, spans, part, delta * parts, limit, parts, (peak, total, acc), block, head_dim)
        for head in range(near):
            if delta == 2:
                write_state(state, head, span, peak[head, 0:1, :], total[head, 0:1, :], acc[head], head_dim)
            else:
                sums[head, :, span] = acc[head]
                stats_out[head, 0:1, span] = peak[head, 0:1, :]
                stats_out[head, 1:2, span] = total[head, 0:1, :]
        return carry

    lax.fori_loop(0, parts, one, 0)


def write_state(state, head, span, peak, total, acc, head_dim):
    state[head, 0:head_dim, span] = acc.astype(BF16)
    width = peak.shape[1]
    index = lax.broadcasted_iota(jnp.int32, (16, width), 0)
    stats = jnp.zeros((16, width), F32)
    for k, piece in enumerate(pieces(peak) + pieces(total)):
        stats = jnp.where(index == k, piece.astype(F32), stats)
    state[head, head_dim : head_dim + 16, span] = stats.astype(BF16)


def merged_state(state, sums, stats, head, span, valid, head_dim):
    factor = math.log2(math.e) / math.sqrt(head_dim)
    arrived = state[head, head_dim : head_dim + 16, span].astype(F32)
    far_peak = jnp.where(valid, arrived[0:1] + arrived[1:2] + arrived[2:3], FLOOR)
    far_total = jnp.where(valid, arrived[3:4] + arrived[4:5] + arrived[5:6], 0.0)
    peak, total = stats[head, 0:1, span], stats[head, 1:2, span]
    high = jnp.maximum(peak, far_peak)
    here = jnp.exp2((peak - high) * factor)
    there = jnp.where(valid, jnp.exp2((far_peak - high) * factor), 0.0)
    acc = sums[head, :, span] * here
    arrived_sum = jnp.where(valid, state[head, 0:head_dim, span].astype(F32), 0.0)
    return high, total * here + far_total * there, acc + arrived_sum * there


def merge_kernel(dims, axis, arrived, sums, stats, state):
    group, _, near, head_dim, block = dims
    valid = lax.axis_index(axis) // group >= 1
    width = sums.shape[2]

    def one(index, carry):
        head = index // (width // block)
        span = pl.ds(pl.multiple_of(lax.rem(index, width // block) * block, block), block)
        peak, total, acc = merged_state(arrived, sums, stats, head, span, valid, head_dim)
        write_state(state, head, span, peak, total, acc, head_dim)
        return carry

    lax.fori_loop(0, near * (width // block), one, 0)


def last_kernel(dims, axis, order, starts, arrived, sums, stats, rows, gain, other, *refs):
    group, slots, near, head_dim, block = dims
    outs, (result, out) = refs[:group], refs[group:]
    row = lax.axis_index(axis) // group
    mine = lax.rem(lax.axis_index(axis), group) * slots
    length = out.shape[1]
    parts = group * length // block
    shards = block // length

    def one(index, carry):
        head = index // parts
        part = lax.rem(index, parts)
        span = pl.ds(pl.multiple_of(part * block, block), block)
        _, total, acc = merged_state(arrived, sums, stats, head, span, row >= 1, head_dim)
        done = (acc / total).astype(BF16).T
        out[pl.ds(part * shards, shards), :, lanes(head, head_dim)] = done.reshape(shards, length, head_dim)
        return carry

    lax.fori_loop(0, parts * near, one, 0)
    scatter_blocks(axis, out, outs)
    width = other.shape[2]
    result[:, :, 0:width] = other[...]
    cross_part(
        out, rows, starts, gain, order, mine, 0, row * group * length, result, head_dim, base=width
    )


def finish_kernel(dims, axis, order, cross, cont, *refs):
    group, slots, near, head_dim = dims
    far_out, near_out, (self_out, cross_out) = refs[:group], refs[group : 2 * group], refs[2 * group :]
    mine = lax.rem(lax.axis_index(axis), group)
    far = slots - near
    for k in range(group):
        first = jnp.bitwise_xor(mine, k) * slots
        for slot in range(slots):
            source, c = (near_out, slot) if slot < near else (far_out, slot - near)
            self_out[:, lanes(order[first + slot], head_dim)] = source[k][:, c * head_dim : (c + 1) * head_dim]
    factor = math.log2(math.e) / math.sqrt(head_dim)
    clen = cont.shape[1]
    row_index = lax.broadcasted_iota(jnp.int32, (clen, clen), 0)
    key_index = lax.broadcasted_iota(jnp.int32, (clen, clen), 1)
    visible = (key_index <= row_index) & (key_index // CLEN == row_index // CLEN)
    for g in range(group):
        for slot in range(slots):
            column = lanes(order[g * slots + slot], head_dim)
            base, c, heads = ((far + 1) * head_dim, slot, near) if slot < near else (0, slot - near, far)
            tail = base + heads * head_dim
            stats = cross[:, g, :, tail : tail + head_dim].astype(F32)
            k = 6 * c
            high = stats[:, :, k : k + 1] + stats[:, :, k + 1 : k + 2] + stats[:, :, k + 2 : k + 3]
            total = stats[:, :, k + 3 : k + 4] + stats[:, :, k + 4 : k + 5] + stats[:, :, k + 5 : k + 6]
            scores = jnp.where(visible, dot(cont[0, :, column], cont[1, :, column], (1, 1)), NEGATIVE)
            final = jnp.maximum(jnp.max(high, axis=0), jnp.max(scores, axis=1, keepdims=True))
            weight = jnp.exp2((high - final[None]) * factor)
            expo = jnp.exp2((scores - final) * factor)
            own = dot(expo.astype(BF16), cont[2, :, column], (1, 0))
            denominator = jnp.sum(weight * total, axis=0) + jnp.sum(expo, axis=1, keepdims=True)
            summed = cross[:, g, :, base + c * head_dim : base + (c + 1) * head_dim].astype(F32) * weight
            merged = jnp.sum(summed, axis=0) + own
            cross_out[:, column] = (merged / denominator).astype(BF16)


def per_device(self_qkv, windows, k_gain, cont_qkv, starts):
    axis = "ctx"
    length, features = self_qkv.shape[1:]
    head_count = windows.shape[0]
    head_dim = features // head_count
    devices = lax.axis_size(axis)
    group = WIN // (2 * length)
    slots = head_count // group
    near = slots // 2
    far = slots - near
    count = devices // group
    block = 2 * length
    rows_here = cont_qkv.shape[1]
    nearby, distant = near * head_dim, far * head_dim
    dims = (group, slots, near, head_dim)
    big = dims + (block,)
    index = jnp.arange(head_count, dtype=jnp.int32)
    above = (windows[None, :] > windows[:, None]) | (
        (windows[None, :] == windows[:, None]) & (index[None, :] < index[:, None])
    )
    rank = jnp.sum(above.astype(jnp.int32), axis=1)
    place = lax.rem(rank, group) * slots + rank // group
    order = jnp.sum(jnp.where(place[None, :] == index[:, None], index[None, :], 0), axis=1)

    def exchange(blocks):
        got = [blocks[0]]
        for k in range(1, group):
            got.append(lax.ppermute(blocks[k], axis, [(source, source ^ k) for source in range(devices)]))
        return got

    def gather(blocks, micros):
        return pl.pallas_call(
            functools.partial(gather_kernel, axis),
            out_shape=jax.ShapeDtypeStruct((group,) + blocks[0].shape, BF16),
            in_specs=[ANY] * group,
            out_specs=VMEM,
            scratch_shapes=[pltpu.SemaphoreType.DMA((group,))],
            cost_estimate=cost(micros),
        compiler_params=GRANT,
        )(*blocks)

    def up(value):
        return lax.ppermute(value, axis, [(k, k + group) for k in range(devices - group)])

    def down(value):
        return lax.ppermute(value, axis, [(k + group, k) for k in range(devices - group)])

    def call(kernel, micros, shapes, *operands, smem=2, **more):
        return pl.pallas_call(
            kernel,
            out_shape=shapes,
            in_specs=[SMEM] * smem + [VMEM] * (len(operands) - smem),
            out_specs=jax.tree.map(lambda _: VMEM, shapes),
            cost_estimate=cost(micros),
        compiler_params=GRANT,
            **more,
        )(*operands)

    def shape(*sizes, dtype=BF16):
        return jax.ShapeDtypeStruct(sizes, dtype)

    packed = pl.pallas_call(
        functools.partial(pack_kernel, dims, axis),
        grid=(3, 2),
        out_shape=(shape(2, length, distant),) * group
        + (shape(length, nearby),) * group
        + (shape(3, length, nearby),) * group,
        in_specs=[SMEM, pl.BlockSpec((1, length // 2, features), lambda i, j: (lax.rem(i + 1, 3), j, 0))],
        out_specs=(
            pl.BlockSpec(
                (1, length // 2, distant), lambda i, j: (jnp.minimum(i, 1), jnp.where(i < 2, j, 1), 0)
            ),
        )
        * group
        + (pl.BlockSpec((length // 2, nearby), lambda i, j: (jnp.where(i < 2, 0, j), 0)),) * group
        + (pl.BlockSpec((1, length // 2, nearby), lambda i, j: (i, j, 0)),) * group,
        name="pack",
        cost_estimate=cost(4),
        compiler_params=GRANT,
    )(order, self_qkv)
    q_near0 = gather(exchange(packed[group : 2 * group]), 1)
    kv_far0 = gather(exchange(packed[:group]), 2)
    rest0 = gather(exchange(packed[2 * group :]), 2)
    rows_sent = call(
        functools.partial(pack_rows_kernel, dims), 2, shape(devices, rows_here, slots * head_dim), order,
        cont_qkv, smem=1,
    )
    rows = lax.all_to_all(rows_sent, axis, 0, 0, tiled=True)
    gain = k_gain.reshape(head_count, head_dim)

    kv_far1 = up(kv_far0)
    q_near1 = down(q_near0)
    half = group // 2
    kv_far2 = up(kv_far1[half:])
    deep = jnp.sum((windows > (group + group - half) * length + 1).astype(jnp.int32)) > group * near
    kv_far3 = lax.cond(deep, lambda value: up(value), lambda value: value, kv_far1[:half])
    q_near2 = down(q_near1)

    state_scratch = [
        pltpu.VMEM((far, 8, block), F32),
        pltpu.VMEM((far, 8, block), F32),
        pltpu.VMEM((far, head_dim, block), F32),
    ]
    state_shape = shape(near, head_dim + 16, group * length)
    local_shape = (shape(near, head_dim, group * length, dtype=F32), shape(near, 8, group * length, dtype=F32))

    def near_step(delta, q, *more):
        return call(
            functools.partial(near_kernel, big, axis, delta, count), 7,
            state_shape if delta == 2 else local_shape, order, windows, q, rest0, *more, scratch_shapes=state_scratch,
        )

    def merge(kernel, micros, shapes, *operands, **more):
        return call(functools.partial(kernel, big, axis), micros, shapes, *operands, **more)

    state2 = up(near_step(2, q_near2))
    state1 = up(merge(merge_kernel, 1, state_shape, state2, *near_step(1, q_near1, rows), smem=0))
    local0 = near_step(0, q_near0)

    def far_call(kernel, micros, shapes, specs, pieces_here, more, *operands):
        return pl.pallas_call(
            functools.partial(kernel, big, axis),
            out_shape=shapes,
            in_specs=specs,
            out_specs=jax.tree.map(lambda _: VMEM, shapes),
            scratch_shapes=more
            + [pltpu.VMEM((pieces_here * group, 2, length, distant), BF16)]
            + state_scratch
            + [pltpu.SemaphoreType.DMA((2,))],
            cost_estimate=cost(micros),
            compiler_params=GRANT,
        )(*operands)

    begun = far_call(
        far_start_kernel, 8,
        (shape(far, head_dim, group * length, dtype=F32), shape(far, 8, group * length, dtype=F32)),
        [SMEM, SMEM, VMEM, ANY, ANY], 2, [], order, windows, rest0, kv_far0, kv_far1,
    )
    *far_out, far_cross = far_call(
        far_kernel, 5,
        (shape(length, distant),) * group + (shape(devices, rows_here, distant + head_dim),),
        [SMEM, SMEM, SMEM, VMEM, VMEM, VMEM, VMEM, VMEM, ANY, ANY], 1,
        [pltpu.VMEM((group, length, distant), BF16)],
        order, windows, starts, rest0, rows, gain, *begun, kv_far2, kv_far3,
    )
    far_back = exchange(far_out)
    *near_out, cross = merge(
        last_kernel, 4,
        (shape(length, nearby),) * group + (shape(devices, rows_here, distant + nearby + 2 * head_dim),),
        order, starts, state1, *local0, rows, gain, far_cross, smem=2,
        scratch_shapes=[pltpu.VMEM((group, length, nearby), BF16)],
    )
    near_back = exchange(near_out)
    cross = lax.all_to_all(cross, axis, 0, 0, tiled=True)
    cross = cross.reshape((count, group) + cross.shape[1:])
    return call(
        functools.partial(finish_kernel, dims, axis), 4, (shape(length, features), shape(rows_here, features)),
        order, cross, cont_qkv, *far_back, *near_back, smem=1,
    )


def solution(mesh):
    in_specs = (
        P(None, ("groups", "ctx"), None),
        P(),
        P(),
        P(None, ("groups", "ctx"), None),
        P("groups"),
    )
    out_specs = (P(("groups", "ctx"), None), P(("groups", "ctx"), None))

    return jax.shard_map(per_device, mesh=mesh, in_specs=in_specs, out_specs=out_specs, check_vma=False)
```
